32 devices in a mesh: row: 1, voc: 32 (over z, y, x, core).
Axes of the slice: x: 2, y: 2, z: 4, core: 2. Of those that a mesh axis runs over, the one named last changes fastest.
Arguments:
- hidden_states: bfloat16 [256, 4096], P('row'), may hold values from -72 to 72
- student_head: bfloat16 [4096, 65536], P('row', 'voc'), may hold values from -2 to 2
- teacher_probs: bfloat16 [256, 81920], P('row', 'voc'), may hold values from 9.9658966e-05 to 1
- block_map: int32 [512, 2], replicated, may hold values from 0 to 639, as said below
- context: int32 [4], P('row'), may hold values from 0 to 3
- map_gates: float32 [4, 512, 2], P(None, 'voc'), may hold values from 0.2 to 5
- map_tiles: bfloat16 [512, 2, 128, 128], P('voc'), may hold values from 0.0009994507 to 1
Outputs:
- grad_logits: bfloat16 [256, 65536], P('row', 'voc')
- head_grad: bfloat16 [4096, 65536], P('row', 'voc')
- kl_loss: float32 [], replicated
The draws below stay inside these ranges and needn't reach their ends.
Inputs may be any that keep to these rules, and one draw needn't show every extreme that they name: `block_map`: in each aligned block of 16 student blocks, at most 2 of the 32 listed ids lie in any one aligned range of 20 teacher blocks, and exactly 2 in one such range.
All inputs are finite; a program needn't handle non-finite values.
Results may differ from the reference program's by a relative error of at most 0.013.
Values may be sent and summed in bfloat16 or wider, within the bound.
A program may use at most 128 MiB of HBM per device.

```python
import math
import jax
import jax.numpy as jnp
from jax import lax

D = 4096
VS = 65536
VT = 81920
BLK = 128
K = 2
NCTX = 4
WIN = 64
TOK_DEV = 256
TOKENS = 256
NBS = 512
NBT = 640
BS_DEV = 16
BT_DEV = 20
NWIN = 4
N_ROW = 1


def draw_hidden_states(key, part):
    values = jax.random.truncated_normal(key, -6.0, 6.0, (TOKENS, D), jnp.float32)
    token_index = jnp.arange(TOKENS, dtype=jnp.int32)
    aligned = token_index % 16 == 5
    level = token_index // 16 % 3
    strength = jnp.where(level == 0, 13.0, jnp.where(level == 1, 20.0, 30.0)).astype(jnp.float32)
    lead = jnp.arange(D, dtype=jnp.int32) < min(8, D)
    chosen = aligned[:, None] & lead[None, :]
    values = jnp.where(chosen, strength[:, None] * jnp.ones((1, D), jnp.float32), values)
    return values.astype(jnp.bfloat16)


def draw_student_head(key, part):
    noise = jax.random.truncated_normal(key, -6.0, 6.0, (D, VS), jnp.float32) * D ** (-0.5)
    lead = (jnp.arange(D, dtype=jnp.int32) < min(8, D))[:, None]
    values = jnp.where(lead, 1.0 + 0.1 * noise, noise)
    return values.astype(jnp.bfloat16)


def draw_block_map(key, part):
    shard_count = NBS // BS_DEV
    entries = BS_DEV * K
    base_count = entries // shard_count
    rank_counts = jnp.full((shard_count,), base_count, jnp.int32)
    rank_counts = rank_counts.at[0].add(1).at[1].add(-1)

    def one_shard(shard):
        shard_key = jax.random.fold_in(key, shard)
        first_key, second_key, third_key = jax.random.split(shard_key, 3)
        source_order = jax.random.permutation(first_key, shard_count)
        source_rank = jnp.repeat(jnp.arange(shard_count, dtype=jnp.int32), rank_counts, total_repeat_length=entries)
        sources = jax.random.permutation(second_key, source_order[source_rank])
        within = jax.random.randint(third_key, (entries,), 0, BT_DEV)
        return (sources * BT_DEV + within).reshape(BS_DEV, K)
    result = jax.vmap(one_shard)(jnp.arange(shard_count, dtype=jnp.int32))
    return result.reshape(NBS, K).astype(jnp.int32)


def plant(values, own_key, low, largest):
    longest = values.shape.index(max(values.shape))
    spots = []
    for shift in (0, 1):
        where = [jax.random.randint(jax.random.fold_in(own_key, axis), (), 0, length) for axis, length in enumerate(values.shape)]
        where[longest] = (where[longest] + shift) % values.shape[longest]
        spots.append(tuple(where))
    return values.at[spots[0]].set(low).at[spots[1]].set(largest)


def levels(rng, dims, cuts, low, high):
    def one(axis_at, blocks):
        steps = jax.random.uniform(jax.random.fold_in(jax.random.fold_in(rng, 6), axis_at), (blocks,), jnp.float32, low / len(cuts), high / len(cuts))
        return jnp.repeat(jnp.exp(steps), dims[axis_at] // blocks).reshape((-1,) + (1,) * (len(dims) - axis_at - 1))

    gain = one(*cuts[0])
    for cut in cuts[1:]:
        gain = gain * one(*cut)
    return gain


def setup_inputs(seed: int = 0) -> dict:
    key_of = jax.random.split(jax.random.key(seed), 8)
    hidden_states = draw_hidden_states(jax.random.fold_in(key_of[7], 71), 0)
    student_head = draw_student_head(jax.random.fold_in(key_of[7], 71), 0)
    teacher_probs = jnp.clip(jnp.exp(math.log(1.0) - 9.213757 * jax.random.uniform(key_of[2], (TOKENS, VT), jnp.float32) ** levels(key_of[2], (TOKENS, VT), ((1, 32),), -0.2, 0.2)), 9.965896606445312e-05, 1.0).astype(jnp.bfloat16)
    block_map = draw_block_map(jax.random.fold_in(key_of[7], 71), 0)
    context = plant(jax.random.randint(key_of[4], (NWIN,), 0, NCTX), jax.random.fold_in(key_of[4], 1), 0, NCTX - 1).astype(jnp.int32)
    map_gates = jnp.clip(jnp.exp(math.log(5.0) - 3.218876 * jax.random.uniform(key_of[5], (NCTX, NBS, K), jnp.float32) ** levels(key_of[5], (NCTX, NBS, K), ((1, 32),), -0.2, 0.2)), 0.2, 5.0)
    map_tiles = jnp.clip(jnp.exp(math.log(1.0) - 6.9083047 * jax.random.uniform(key_of[6], (NBS, K, BLK, BLK), jnp.float32) ** levels(key_of[6], (NBS, K, BLK, BLK), ((0, 32),), -0.2, 0.2)), 0.0009994507, 1.0).astype(jnp.bfloat16)
    return dict(hidden_states=hidden_states, student_head=student_head, teacher_probs=teacher_probs, block_map=block_map, context=context, map_gates=map_gates, map_tiles=map_tiles)


def reference(hidden_states, student_head, teacher_probs, block_map, context, map_gates, map_tiles):
    logits = jnp.dot(hidden_states, student_head, preferred_element_type=jnp.float32)
    peak = lax.optimization_barrier(jnp.max(logits, axis=1, keepdims=True))
    log_norm = peak + jnp.log(lax.optimization_barrier(jnp.sum(jnp.exp(logits - peak), axis=1, keepdims=True)))
    token_context = jnp.repeat(context, WIN)
    teacher_blocks = teacher_probs.reshape(TOKENS, NBT, BLK)
    gate_token = map_gates[token_context]
    stride = math.gcd(NBS, 16)

    def map_block(block_index):
        first_block = (block_index * stride).astype(jnp.int32)
        wanted = lax.dynamic_slice_in_dim(block_map, first_block, stride, 0)
        pieces = jnp.take(teacher_blocks, wanted.reshape(-1), axis=1).reshape(TOKENS, stride, K, BLK).astype(jnp.float32)
        tile_part = lax.dynamic_slice_in_dim(map_tiles, first_block, stride, 0).astype(jnp.float32)
        products = jnp.einsum('tbkj,bkjc->tbkc', pieces, tile_part)
        gate_part = lax.dynamic_slice_in_dim(gate_token, first_block, stride, 1)
        return lax.optimization_barrier(jnp.sum(gate_part[..., None] * products, axis=2))
    mapped = lax.map(map_block, jnp.arange(NBS // stride, dtype=jnp.int32))
    mapped = jnp.moveaxis(mapped, 0, 1).reshape(TOKENS, VS)
    row_total = lax.optimization_barrier(jnp.sum(mapped, axis=1, keepdims=True))
    target = mapped / row_total
    grad_logits = (VS * (jnp.exp(logits - log_norm) - target)).astype(jnp.bfloat16)
    kl_loss = jnp.sum(target * (jnp.log(target) - logits + log_norm)) / TOKENS
    inv_root = 1.0 / math.sqrt(TOKENS)
    column_width = math.gcd(VS, 4096)

    def grad_columns(column_index):
        first_column = (column_index * column_width).astype(jnp.int32)
        grad_part = lax.dynamic_slice_in_dim(grad_logits, first_column, column_width, 1)
        running = jnp.zeros((D, column_width), jnp.float32)
        for group in range(N_ROW):
            hidden_group = hidden_states[group * TOK_DEV:(group + 1) * TOK_DEV]
            grad_group = grad_part[group * TOK_DEV:(group + 1) * TOK_DEV]
            part_value = jnp.dot(hidden_group.T, grad_group, preferred_element_type=jnp.float32) * inv_root
            part_value = lax.optimization_barrier(part_value.astype(jnp.bfloat16))
            running = running + part_value.astype(jnp.float32)
        return running.astype(jnp.bfloat16)
    stacked = lax.map(grad_columns, jnp.arange(VS // column_width, dtype=jnp.int32))
    head_grad = jnp.moveaxis(stacked, 0, 1).reshape(D, VS)
    return (grad_logits, head_grad, kl_loss)
```

```python
import functools
import math

import jax
import jax.numpy as jnp
from jax import lax
from jax.experimental import pallas as pl
from jax.experimental.pallas import tpu as pltpu
from jax.sharding import PartitionSpec as P

MESH = pl.DeviceIdType.MESH
CHUNKS = 8


def exchange_kernel(
    n,
    map_hbm,
    context_hbm,
    gates_hbm,
    hidden_hbm,
    head_hbm,
    teacher_hbm,
    tiles_hbm,
    logits_ref,
    mapped_ref,
    turned_ref,
    cols_ref,
    map_vec,
    map_ref,
    context_ref,
    gates_ref,
    take_vec,
    take_ref,
    slot_vec,
    slot_ref,
    hidden_ref,
    head_ref,
    tiles_ref,
    shelf,
    outgoing,
    incoming,
    extra,
    landing,
    products,
    stats_out,
    stats_in,
    local_sem,
    head_sem,
    send_sem,
    recv_sem,
    extra_send,
    extra_recv,
    stat_send,
    stat_recv,
):
    me = lax.axis_index("voc")
    levels = n.bit_length() - 1
    bits = [(me // 2**b) % 2 for b in range(levels)]
    flips = [(1 - 2 * bits[b]) * 2**b for b in range(levels)]
    tokens, width = hidden_ref.shape
    entries, block, _ = tiles_ref.shape
    fanout = map_vec.shape[0]
    blocks = entries // fanout
    per = shelf.shape[0] - 1
    windows = context_ref.shape[0]
    chunk = logits_ref.shape[1] // CHUNKS
    rows = width // CHUNKS
    stride = 1 << per.bit_length()

    def partner(d):
        return me + sum(flips[b] for b in range(levels) if (d >> b) & 1)

    def reverse(e):
        return sum(((e // 2**b) % 2) * 2 ** (levels - 1 - b) for b in range(levels))

    order = list(range(1, n))
    load_map = pltpu.make_async_copy(map_hbm, map_vec, local_sem.at[0])
    load_ids = pltpu.make_async_copy(map_hbm, map_ref, local_sem.at[1])
    load_context = pltpu.make_async_copy(context_hbm, context_ref, local_sem.at[2])
    load_gates = pltpu.make_async_copy(gates_hbm, gates_ref, local_sem.at[3])
    load_hidden = pltpu.make_async_copy(hidden_hbm, hidden_ref, local_sem.at[4])
    load_tiles = pltpu.make_async_copy(tiles_hbm, tiles_ref, local_sem.at[5])
    move_take = pltpu.make_async_copy(take_vec, take_ref, local_sem.at[6])
    move_slot = pltpu.make_async_copy(slot_vec, slot_ref, local_sem.at[7])

    def load_shelf(i):
        return pltpu.make_async_copy(
            teacher_hbm.at[:, pl.ds(i * block, block)], shelf.at[i], local_sem.at[8 + i]
        )

    def load_head(c):
        part = pl.ds(pl.multiple_of(c * chunk, chunk), chunk)
        return pltpu.make_async_copy(head_hbm.at[:, part], head_ref.at[:, part], head_sem.at[c])

    def main_copy(d):
        return pltpu.make_async_remote_copy(
            src_ref=outgoing.at[partner(d)],
            dst_ref=incoming.at[me],
            send_sem=send_sem.at[d],
            recv_sem=recv_sem.at[d],
            device_id={"voc": partner(d)},
            device_id_type=MESH,
        )

    def main_recv(d):
        return pltpu.make_async_remote_copy(
            src_ref=outgoing.at[partner(d)],
            dst_ref=incoming.at[partner(d)],
            send_sem=send_sem.at[d],
            recv_sem=recv_sem.at[d],
            device_id={"voc": partner(d)},
            device_id_type=MESH,
        )

    def region(s):
        return sum(bits[b] * (n >> (b + 1)) for b in range(s))

    def extra_copy(s):
        half = n >> (s + 1)
        away = region(s) + (1 - bits[s]) * half
        return pltpu.make_async_remote_copy(
            src_ref=extra.at[pl.ds(away, half)],
            dst_ref=landing.at[pl.ds(n - 2 * half, half)],
            send_sem=extra_send.at[s],
            recv_sem=extra_recv.at[s],
            device_id={"voc": partner(1 << s)},
            device_id_type=MESH,
        )

    def extra_finish(s):
        half = n >> (s + 1)
        kept = region(s) + bits[s] * half
        extra_copy(s).wait()

        def add(i, carry):
            extra[kept + i] = extra[kept + i] + landing[n - 2 * half + i]
            return carry

        lax.fori_loop(0, half, add, 0)
        if s + 1 < levels:
            extra_copy(s + 1).start()
        else:
            incoming[n] = extra[region(levels)]

    def stat_copy(d, owner):
        return pltpu.make_async_remote_copy(
            src_ref=stats_out,
            dst_ref=stats_in.at[owner],
            send_sem=stat_send.at[d],
            recv_sem=stat_recv.at[d],
            device_id={"voc": partner(d)},
            device_id_type=MESH,
        )

    load_map.start()
    for i in range(per):
        load_shelf(i).start()
    barrier = pltpu.get_barrier_semaphore()
    for d in reversed(order):
        pl.semaphore_signal(barrier, inc=1, device_id={"voc": partner(d)}, device_id_type=MESH)
    load_ids.start()
    load_context.start()
    load_gates.start()
    load_hidden.start()
    load_tiles.start()

    load_map.wait()
    listed = map_vec[...]
    count = listed.shape[1]
    place = lax.broadcasted_iota(jnp.int32, listed.shape, 0) * blocks + (
        lax.broadcasted_iota(jnp.int32, listed.shape, 1) % blocks
    )
    offset = listed - me * per
    owned = (offset >= 0) & (offset < per)
    key = place * stride + offset
    big = entries * stride
    first = jnp.min(jnp.where(owned, key, big), axis=0, keepdims=True)
    last = jnp.max(jnp.where(owned, key, -1), axis=0, keepdims=True)
    shift = 1
    while shift < blocks:
        first = jnp.minimum(first, pltpu.roll(first, count - shift, 1))
        last = jnp.maximum(last, pltpu.roll(last, count - shift, 1))
        shift *= 2
    take_vec[0:1, :] = first & (stride - 1)
    take_vec[1:2, :] = jnp.where(last > first, last & (stride - 1), per)
    move_take.start()
    shelf[per] = jnp.zeros(shelf.shape[1:], shelf.dtype)
    move_take.wait()
    for i in range(per):
        load_shelf(i).wait()

    def fill(e, carry):
        outgoing[e] = shelf[take_ref[0, e * blocks]]
        extra[reverse(e)] = shelf[take_ref[1, e * blocks]]
        return carry

    lax.fori_loop(0, n, fill, 0)
    pl.semaphore_wait(barrier, n - 1)
    extra_copy(0).start()
    for d in order:
        main_copy(d).start()
    incoming[me] = outgoing[me]
    for c in range(CHUNKS):
        load_head(c).start()

    load_ids.wait()
    lane = lax.broadcasted_iota(jnp.int32, (1, block), 1)
    low = lane * per
    own_first = jnp.full((1, block), entries, jnp.int32)
    own_second = jnp.full((1, block), -1, jnp.int32)
    for p in reversed(range(entries)):
        wanted = map_ref[p // blocks, me * blocks + p % blocks]
        hit = (wanted >= low) & (wanted < low + per) & (lane < n)
        own_second = jnp.where(hit & (own_first < entries), own_first, own_second)
        own_first = jnp.where(hit, p, own_first)
    doubled = jnp.max(own_second, axis=1, keepdims=True)
    chosen = jnp.where(lane == n, doubled, own_first)
    slot_vec[...] = jnp.where(chosen < entries, chosen, 0)
    move_slot.start()
    move_slot.wait()
    load_context.wait()
    load_gates.wait()
    load_hidden.wait()

    def column(c, carry):
        load_head(c).wait()
        part = pl.ds(pl.multiple_of(c * chunk, chunk), chunk)
        logits_ref[:, part] = jnp.dot(
            hidden_ref[...], head_ref[:, part], preferred_element_type=jnp.float32
        )
        return carry

    def turn(c, carry):
        span = pl.ds(pl.multiple_of(c * rows, rows), rows)
        turned_ref[span, :] = hidden_ref[:, span].T
        return carry

    def multiply(slot):
        place = slot_ref[0, slot]
        k = place // blocks
        b = place - k * blocks
        value = jnp.dot(
            incoming[slot], tiles_ref[b * fanout + k], preferred_element_type=jnp.float32
        )
        span = tokens // windows
        for w in range(windows):
            gate = gates_ref[context_ref[w], k, b]
            products[slot, w * span : (w + 1) * span] = value[w * span : (w + 1) * span] * gate

    lax.fori_loop(0, CHUNKS, column, 0)
    extra_finish(0)
    lax.fori_loop(0, CHUNKS, turn, 0)
    peak = jnp.max(logits_ref[...], axis=1, keepdims=True)
    summed = jnp.sum(jnp.exp(logits_ref[...] - peak), axis=1, keepdims=True)
    load_tiles.wait()
    multiply(me)
    done = 0
    for s in range(1, levels):
        extra_finish(s)
        upto = s * (len(order) // 2) // levels
        for d in order[done:upto]:
            main_recv(d).wait_recv()
            multiply(partner(d))
        done = upto
    multiply(n)
    for d in order[done:]:
        main_recv(d).wait_recv()
        multiply(partner(d))

    total = jnp.zeros((tokens, block), jnp.float32)
    cross = jnp.zeros((tokens, block), jnp.float32)
    for b in range(blocks):
        value = None
        for k in range(fanout):
            p = k * blocks + b
            wanted = map_ref[k, me * blocks + b]
            source = wanted // per
            slot = jnp.where(slot_ref[0, source] == p, source, n)
            part = products[slot]
            value = part if value is None else value + part
        mapped_ref[:, b * block : (b + 1) * block] = value
        total = total + value
        cross = cross + value * (
            jnp.log(value) - (logits_ref[:, b * block : (b + 1) * block] - peak)
        )
    total = jnp.sum(total, axis=1, keepdims=True)
    cross = jnp.sum(cross, axis=1, keepdims=True)
    lanes = lax.broadcasted_iota(jnp.int32, (tokens, block), 1)
    packed = jnp.where(
        lanes == 0, peak, jnp.where(lanes == 1, summed, jnp.where(lanes == 2, total, cross))
    )
    stats_out[...] = packed.T[: stats_out.shape[0]]
    stats_in[me] = stats_out[...]
    for d in reversed(order):
        stat_copy(d, me).start()
    for d in order:
        main_copy(d).wait_send()
    for d in reversed(order):
        stat_copy(d, partner(d)).wait_recv()
    peaks = stats_in[:, 0, :]
    sums = stats_in[:, 1, :]
    totals = stats_in[:, 2, :]
    crosses = stats_in[:, 3, :]
    top = jnp.max(peaks, axis=0, keepdims=True)
    log_norm = top + jnp.log(jnp.sum(sums * jnp.exp(peaks - top), axis=0, keepdims=True))
    row_total = jnp.sum(totals, axis=0, keepdims=True)
    weighted = jnp.sum(crosses + totals * (log_norm - peaks), axis=0, keepdims=True)
    divergence = weighted / row_total - jnp.log(row_total)
    divergence = jnp.sum(divergence, axis=1, keepdims=True)
    line = lax.broadcasted_iota(jnp.int32, (block, tokens), 0)
    cols_ref[...] = jnp.where(
        line == 0, log_norm, jnp.where(line == 1, 1.0 / row_total, divergence)
    ).T
    for d in order:
        stat_copy(d, me).wait_send()


def exchange(hidden, head, teacher, block_map, context, gates, tiles):
    n = lax.axis_size("voc")
    tokens, width = hidden.shape
    cols = head.shape[1]
    block = tiles.shape[-1]
    per = teacher.shape[1] // block
    levels = n.bit_length() - 1
    hbm = pl.BlockSpec(memory_space=pl.ANY)
    vmem = pl.BlockSpec(memory_space=pltpu.VMEM)
    return pl.pallas_call(
        functools.partial(exchange_kernel, n),
        out_shape=(
            pltpu.VMEM((tokens, cols), jnp.float32),
            pltpu.VMEM((tokens, cols), jnp.float32),
            pltpu.VMEM((width, tokens), hidden.dtype),
            pltpu.VMEM((tokens, block), jnp.float32),
        ),
        in_specs=[hbm] * 7,
        out_specs=(vmem,) * 4,
        scratch_shapes=[
            pltpu.VMEM(block_map.shape, jnp.int32),
            pltpu.SMEM(block_map.shape, jnp.int32),
            pltpu.SMEM(context.shape, jnp.int32),
            pltpu.SMEM(gates.shape, jnp.float32),
            pltpu.VMEM((2, block_map.shape[1]), jnp.int32),
            pltpu.SMEM((2, block_map.shape[1]), jnp.int32),
            pltpu.VMEM((1, block), jnp.int32),
            pltpu.SMEM((1, block), jnp.int32),
            pltpu.VMEM((tokens, width), hidden.dtype),
            pltpu.VMEM(head.shape, head.dtype),
            pltpu.VMEM(tiles.shape, tiles.dtype),
            pltpu.VMEM((per + 1, tokens, block), teacher.dtype),
            pltpu.VMEM((n, tokens, block), teacher.dtype),
            pltpu.VMEM((n + 1, tokens, block), teacher.dtype),
            pltpu.VMEM((n, tokens, block), teacher.dtype),
            pltpu.VMEM((n, tokens, block), teacher.dtype),
            pltpu.VMEM((n + 1, tokens, block), jnp.float32),
            pltpu.VMEM((4, tokens), jnp.float32),
            pltpu.VMEM((n, 4, tokens), jnp.float32),
            pltpu.SemaphoreType.DMA((8 + per,)),
            pltpu.SemaphoreType.DMA((CHUNKS,)),
            pltpu.SemaphoreType.DMA((n,)),
            pltpu.SemaphoreType.DMA((n,)),
            pltpu.SemaphoreType.DMA((levels,)),
            pltpu.SemaphoreType.DMA((levels,)),
            pltpu.SemaphoreType.DMA((n,)),
            pltpu.SemaphoreType.DMA((n,)),
        ],
        compiler_params=pltpu.CompilerParams(
            collective_id=0, has_side_effects=True, vmem_limit_bytes=48 << 20
        ),
        name="exchange",
    )(block_map, context, gates, hidden, head, teacher, tiles)


def gradient_kernel(
    vocab,
    inv_root,
    rows,
    cols_ref,
    logits_ref,
    mapped_ref,
    turned_ref,
    grad_hbm,
    out_hbm,
    kl_ref,
    grad_ref,
    out_ref,
    grad_sem,
    out_sem,
):
    chunk = grad_ref.shape[1] // CHUNKS
    log_norm = cols_ref[:, 0:1]
    inverse = cols_ref[:, 1:2]

    def save_grad(c):
        part = pl.ds(pl.multiple_of(c * chunk, chunk), chunk)
        return pltpu.make_async_copy(grad_ref.at[:, part], grad_hbm.at[:, part], grad_sem.at[c])

    def save_out(c):
        part = pl.ds(pl.multiple_of(c * chunk, chunk), chunk)
        return pltpu.make_async_copy(out_ref.at[:, part], out_hbm.at[:, part], out_sem.at[c])

    def column(c, carry):
        part = pl.ds(pl.multiple_of(c * chunk, chunk), chunk)
        grad = (
            vocab * (jnp.exp(logits_ref[:, part] - log_norm) - mapped_ref[:, part] * inverse)
        ).astype(grad_ref.dtype)
        grad_ref[:, part] = grad
        save_grad(c).start()
        out_ref[:, part] = (
            jnp.dot(turned_ref[...], grad, preferred_element_type=jnp.float32) * inv_root
        ).astype(out_ref.dtype)
        save_out(c).start()
        return carry

    lax.fori_loop(0, CHUNKS, column, 0)
    kl_ref[0, 0] = jnp.max(cols_ref[0:1, 2:3]) * (1.0 / rows)

    def drain(c, carry):
        save_grad(c).wait()
        save_out(c).wait()
        return carry

    lax.fori_loop(0, CHUNKS, drain, 0)


def gradients(logits, mapped, turned, cols, vocab, inv_root, rows):
    tokens, columns = logits.shape
    width = turned.shape[0]
    hbm = pl.BlockSpec(memory_space=pl.ANY)
    vmem = pl.BlockSpec(memory_space=pltpu.VMEM)
    return pl.pallas_call(
        functools.partial(gradient_kernel, float(vocab), inv_root, rows),
        out_shape=(
            jax.ShapeDtypeStruct((tokens, columns), jnp.bfloat16),
            jax.ShapeDtypeStruct((width, columns), jnp.bfloat16),
            jax.ShapeDtypeStruct((1, 1), jnp.float32),
        ),
        in_specs=[vmem] * 4,
        out_specs=(hbm, hbm, pl.BlockSpec(memory_space=pltpu.SMEM)),
        scratch_shapes=[
            pltpu.VMEM((tokens, columns), jnp.bfloat16),
            pltpu.VMEM((width, columns), jnp.bfloat16),
            pltpu.SemaphoreType.DMA((CHUNKS,)),
            pltpu.SemaphoreType.DMA((CHUNKS,)),
        ],
        compiler_params=pltpu.CompilerParams(vmem_limit_bytes=40 << 20),
        name="gradients",
    )(cols, logits, mapped, turned)


def per_device(
    hidden_states, student_head, teacher_probs, block_map, context, map_gates, map_tiles
):
    voc_count = lax.axis_size("voc")
    rows_total = hidden_states.shape[0] * lax.axis_size("row")
    inv_root = 1.0 / math.sqrt(rows_total)
    vocab_total = student_head.shape[1] * voc_count
    blocks, fanout, block, _ = map_tiles.shape
    head = lax.all_gather(student_head, "row", axis=0, tiled=True)
    logits, mapped, turned, cols = exchange(
        hidden_states,
        head,
        teacher_probs,
        block_map.T,
        context,
        map_gates.transpose(0, 2, 1),
        map_tiles.reshape(blocks * fanout, block, block),
    )
    grad_logits, head_part, kl = gradients(
        logits, mapped, turned, cols, vocab_total, inv_root, rows_total
    )
    kl_loss = lax.psum(kl.reshape(()), "row")
    head_grad = lax.psum_scatter(head_part, "row", scatter_dimension=0, tiled=True)
    return (grad_logits, head_grad, kl_loss)


def solution(mesh):
    placed = (
        P("row", None),
        P("row", "voc"),
        P("row", "voc"),
        P(),
        P("row"),
        P(None, "voc", None),
        P("voc", None, None, None),
    )
    return jax.shard_map(
        per_device,
        mesh=mesh,
        in_specs=placed,
        out_specs=(P("row", "voc"), P("row", "voc"), P()),
        check_vma=False,
    )
```

```python
import functools
import math

import jax
import jax.numpy as jnp
from jax import lax
from jax.experimental import pallas as pl
from jax.experimental.pallas import tpu as pltpu
from jax.sharding import PartitionSpec as P

MESH = pl.DeviceIdType.MESH
CHUNKS = 8
PIECES = 4
SPLITS = 4


def exchange_kernel(
    n,
    vocab,
    map_hbm,
    context_hbm,
    gates_hbm,
    hidden_hbm,
    head_hbm,
    teacher_hbm,
    tiles_hbm,
    scaled_ref,
    mapped_ref,
    turned_ref,
    cols_ref,
    map_vec,
    map_ref,
    context_ref,
    gates_ref,
    take_vec,
    take_ref,
    slot_vec,
    slot_ref,
    hidden_ref,
    head_ref,
    tiles_ref,
    shelf,
    outgoing,
    incoming,
    extra,
    landing,
    products,
    logits_ref,
    sums_ref,
    norm_out,
    norm_in,
    stats_out,
    stats_in,
    local_sem,
    head_sem,
    send_sem,
    recv_sem,
    extra_send,
    extra_recv,
    norm_send,
    norm_recv,
    stat_send,
    stat_recv,
):
    me = lax.axis_index("voc")
    levels = n.bit_length() - 1
    bits = [(me // 2**b) % 2 for b in range(levels)]
    flips = [(1 - 2 * bits[b]) * 2**b for b in range(levels)]
    tokens, width = hidden_ref.shape
    entries, block, _ = tiles_ref.shape
    fanout = map_vec.shape[0]
    blocks = entries // fanout
    per = shelf.shape[0] - 1
    windows = context_ref.shape[0]
    chunk = scaled_ref.shape[1] // CHUNKS
    rows = width // CHUNKS
    stride = 1 << per.bit_length()

    def partner(d):
        return me + sum(flips[b] for b in range(levels) if (d >> b) & 1)

    def reverse(e):
        return sum(((e // 2**b) % 2) * 2 ** (levels - 1 - b) for b in range(levels))

    order = list(range(1, n))
    load_map = pltpu.make_async_copy(map_hbm, map_vec, local_sem.at[0])
    load_ids = pltpu.make_async_copy(map_hbm, map_ref, local_sem.at[1])
    load_context = pltpu.make_async_copy(context_hbm, context_ref, local_sem.at[2])
    load_gates = pltpu.make_async_copy(gates_hbm, gates_ref, local_sem.at[3])
    load_hidden = pltpu.make_async_copy(hidden_hbm, hidden_ref, local_sem.at[4])
    load_tiles = pltpu.make_async_copy(tiles_hbm, tiles_ref, local_sem.at[5])
    move_take = pltpu.make_async_copy(take_vec, take_ref, local_sem.at[6])
    move_slot = pltpu.make_async_copy(slot_vec, slot_ref, local_sem.at[7])

    def load_shelf(i):
        return pltpu.make_async_copy(
            teacher_hbm.at[:, pl.ds(i * block, block)], shelf.at[i], local_sem.at[8 + i]
        )

    def load_head(c):
        part = pl.ds(pl.multiple_of(c * chunk, chunk), chunk)
        return pltpu.make_async_copy(head_hbm.at[:, part], head_ref.at[:, part], head_sem.at[c])

    def main_copy(d):
        return pltpu.make_async_remote_copy(
            src_ref=outgoing.at[partner(d)],
            dst_ref=incoming.at[me],
            send_sem=send_sem.at[d],
            recv_sem=recv_sem.at[d],
            device_id={"voc": partner(d)},
            device_id_type=MESH,
        )

    def main_recv(d):
        return pltpu.make_async_remote_copy(
            src_ref=outgoing.at[partner(d)],
            dst_ref=incoming.at[partner(d)],
            send_sem=send_sem.at[d],
            recv_sem=recv_sem.at[d],
            device_id={"voc": partner(d)},
            device_id_type=MESH,
        )

    def region(s):
        return sum(bits[b] * (n >> (b + 1)) for b in range(s))

    def extra_copy(s):
        half = n >> (s + 1)
        away = region(s) + (1 - bits[s]) * half
        return pltpu.make_async_remote_copy(
            src_ref=extra.at[pl.ds(away, half)],
            dst_ref=landing.at[pl.ds(n - 2 * half, half)],
            send_sem=extra_send.at[s],
            recv_sem=extra_recv.at[s],
            device_id={"voc": partner(1 << s)},
            device_id_type=MESH,
        )

    def extra_finish(s):
        half = n >> (s + 1)
        kept = region(s) + bits[s] * half
        extra_copy(s).wait()

        def add(i, carry):
            extra[kept + i] = extra[kept + i] + landing[n - 2 * half + i]
            return carry

        lax.fori_loop(0, half, add, 0)
        if s + 1 < levels:
            extra_copy(s + 1).start()
        else:
            incoming[n] = extra[region(levels)]

    def norm_copy(s):
        return pltpu.make_async_remote_copy(
            src_ref=norm_out.at[s],
            dst_ref=norm_in.at[s],
            send_sem=norm_send.at[s],
            recv_sem=norm_recv.at[s],
            device_id={"voc": partner(1 << s)},
            device_id_type=MESH,
        )

    def norm_merge(s):
        norm_copy(s).wait()
        mine, other = norm_out[s, 0:1, :], norm_in[s, 0:1, :]
        top = jnp.maximum(mine, other)
        merged = norm_out[s, 1:2, :] * jnp.exp(mine - top)
        merged = merged + norm_in[s, 1:2, :] * jnp.exp(other - top)
        return top, merged

    def norm_step(s):
        top, merged = norm_merge(s)
        norm_out[s + 1, 0:1, :] = top
        norm_out[s + 1, 1:2, :] = merged
        norm_copy(s + 1).start()

    def stat_copy(d, owner):
        return pltpu.make_async_remote_copy(
            src_ref=stats_out,
            dst_ref=stats_in.at[owner],
            send_sem=stat_send.at[d],
            recv_sem=stat_recv.at[d],
            device_id={"voc": partner(d)},
            device_id_type=MESH,
        )

    load_map.start()
    for i in range(per):
        load_shelf(i).start()
    barrier = pltpu.get_barrier_semaphore()
    for d in reversed(order):
        pl.semaphore_signal(barrier, inc=1, device_id={"voc": partner(d)}, device_id_type=MESH)
    load_ids.start()
    load_context.start()
    load_gates.start()
    load_hidden.start()
    load_tiles.start()

    load_map.wait()
    listed = map_vec[...]
    count = listed.shape[1]
    place = lax.broadcasted_iota(jnp.int32, listed.shape, 0) * blocks + (
        lax.broadcasted_iota(jnp.int32, listed.shape, 1) % blocks
    )
    offset = listed - me * per
    owned = (offset >= 0) & (offset < per)
    key = place * stride + offset
    big = entries * stride
    first = jnp.min(jnp.where(owned, key, big), axis=0, keepdims=True)
    last = jnp.max(jnp.where(owned, key, -1), axis=0, keepdims=True)
    shift = 1
    while shift < blocks:
        first = jnp.minimum(first, pltpu.roll(first, count - shift, 1))
        last = jnp.maximum(last, pltpu.roll(last, count - shift, 1))
        shift *= 2
    take_vec[0:1, :] = first & (stride - 1)
    take_vec[1:2, :] = jnp.where(last > first, last & (stride - 1), per)
    move_take.start()
    shelf[per] = jnp.zeros(shelf.shape[1:], shelf.dtype)
    move_take.wait()
    for i in range(per):
        load_shelf(i).wait()

    def fill(e, carry):
        outgoing[e] = shelf[take_ref[0, e * blocks]]
        extra[reverse(e)] = shelf[take_ref[1, e * blocks]]
        return carry

    lax.fori_loop(0, n, fill, 0)
    pl.semaphore_wait(barrier, n - 1)
    extra_copy(0).start()
    for d in order:
        main_copy(d).start()
    incoming[me] = outgoing[me]
    for c in range(CHUNKS):
        load_head(c).start()

    load_ids.wait()
    lane = lax.broadcasted_iota(jnp.int32, (1, block), 1)
    low = lane * per
    own_first = jnp.full((1, block), entries, jnp.int32)
    own_second = jnp.full((1, block), -1, jnp.int32)
    for p in reversed(range(entries)):
        wanted = map_ref[p // blocks, me * blocks + p % blocks]
        hit = (wanted >= low) & (wanted < low + per) & (lane < n)
        own_second = jnp.where(hit & (own_first < entries), own_first, own_second)
        own_first = jnp.where(hit, p, own_first)
    doubled = jnp.max(own_second, axis=1, keepdims=True)
    chosen = jnp.where(lane == n, doubled, own_first)
    slot_vec[...] = jnp.where(chosen < entries, chosen, 0)
    move_slot.start()
    move_slot.wait()
    load_context.wait()
    load_gates.wait()
    load_hidden.wait()

    def column(c, carry):
        load_head(c).wait()
        part = pl.ds(pl.multiple_of(c * chunk, chunk), chunk)
        logits_ref[:, part] = jnp.dot(
            hidden_ref[...], head_ref[:, part], preferred_element_type=jnp.float32
        )
        return carry

    def turn(c, carry):
        span = pl.ds(pl.multiple_of(c * rows, rows), rows)
        turned_ref[span, :] = hidden_ref[:, span].T
        return carry

    def multiply(slot):
        place = slot_ref[0, slot]
        k = place // blocks
        b = place - k * blocks
        value = jnp.dot(
            incoming[slot], tiles_ref[b * fanout + k], preferred_element_type=jnp.float32
        )
        span = tokens // windows
        for w in range(windows):
            gate = gates_ref[context_ref[w], k, b]
            products[slot, w * span : (w + 1) * span] = value[w * span : (w + 1) * span] * gate

    def take(group):
        for d in group:
            main_recv(d).wait_recv()
        for d in group:
            multiply(partner(d))

    early = CHUNKS // 3
    lax.fori_loop(0, early, column, 0)
    extra_finish(0)
    lax.fori_loop(early, CHUNKS, column, 0)
    lanes = lax.broadcasted_iota(jnp.int32, (tokens, block), 1)
    peak = jnp.max(logits_ref[...], axis=1, keepdims=True)
    summed = jnp.sum(jnp.exp(logits_ref[...] - peak), axis=1, keepdims=True)
    norm_out[0] = jnp.where(lanes == 0, peak, summed).T[:2]
    norm_copy(0).start()
    lax.fori_loop(0, CHUNKS, turn, 0)
    load_tiles.wait()
    near = order[: n // 2 - 1]
    far = order[n // 2 - 1 :]
    half = len(near) // 2
    norm_step(0)
    multiply(me)
    for s in range(1, levels - 1):
        extra_finish(s)
        if s < levels - 2:
            norm_step(s)
        if s == levels - 3:
            take(near[:half])
            norm_step(s + 1)
        if s == levels - 2:
            take(near[half:])
    top, merged = norm_merge(levels - 1)
    log_norm = top + jnp.log(merged)
    line = lax.broadcasted_iota(jnp.int32, (block, tokens), 0)
    cols_ref[...] = jnp.where(line == 0, log_norm, 0.0).T

    def scale(c, carry):
        part = pl.ds(pl.multiple_of(c * chunk, chunk), chunk)
        centred = logits_ref[:, part] - cols_ref[:, 0:1]
        logits_ref[:, part] = centred
        scaled_ref[:, part] = vocab * jnp.exp(centred)
        return carry

    lax.fori_loop(0, CHUNKS, scale, 0)
    extra_finish(levels - 1)
    multiply(n)
    quarter = len(far) // 2
    for i in range(0, len(far), quarter):
        take(far[i : i + quarter])

    slots = []
    for b in range(blocks):
        for k in range(fanout):
            source = map_ref[k, me * blocks + b] // per
            slots.append(jnp.where(slot_ref[0, source] == k * blocks + b, source, n))
    strip = sums_ref.shape[0] // CHUNKS
    strip_lane = lax.broadcasted_iota(jnp.int32, (strip, block), 1)

    def combine(i, carry):
        span = pl.ds(pl.multiple_of(i * strip, strip), strip)
        total = jnp.zeros((strip, block), jnp.float32)
        cross = jnp.zeros((strip, block), jnp.float32)
        for b in range(blocks):
            value = products[slots[b * fanout], span]
            for k in range(1, fanout):
                value = value + products[slots[b * fanout + k], span]
            part = slice(b * block, (b + 1) * block)
            mapped_ref[span, part] = value
            total = total + value
            cross = cross + value * (jnp.log(value) - logits_ref[span, part])
        total = jnp.sum(total, axis=1, keepdims=True)
        cross = jnp.sum(cross, axis=1, keepdims=True)
        sums_ref[span, :] = jnp.where(strip_lane == 0, total, cross)
        return carry

    lax.fori_loop(0, CHUNKS, combine, 0)
    stats_out[...] = sums_ref[...].T[:2]
    for d in reversed(order):
        stat_copy(d, me).start()
    stats_in[me] = stats_out[...]
    for d in order:
        main_copy(d).wait_send()
    for d in reversed(order):
        stat_copy(d, partner(d)).wait_recv()
    row_total = jnp.sum(stats_in[:, 0, :], axis=0, keepdims=True)
    crosses = jnp.sum(stats_in[:, 1, :], axis=0, keepdims=True)
    divergence = crosses / row_total - jnp.log(row_total)
    divergence = jnp.sum(divergence, axis=1, keepdims=True)
    cols_ref[...] = jnp.where(line == 0, vocab / row_total, divergence).T
    for d in order:
        stat_copy(d, me).wait_send()


def exchange(hidden, head, teacher, block_map, context, gates, tiles, vocab):
    n = lax.axis_size("voc")
    tokens, width = hidden.shape
    cols = head.shape[1]
    block = tiles.shape[-1]
    per = teacher.shape[1] // block
    levels = n.bit_length() - 1
    hbm = pl.BlockSpec(memory_space=pl.ANY)
    vmem = pl.BlockSpec(memory_space=pltpu.VMEM)
    return pl.pallas_call(
        functools.partial(exchange_kernel, n, float(vocab)),
        out_shape=(
            pltpu.VMEM((tokens, cols), jnp.float32),
            pltpu.VMEM((tokens, cols), jnp.float32),
            pltpu.VMEM((width, tokens), hidden.dtype),
            pltpu.VMEM((tokens, block), jnp.float32),
        ),
        in_specs=[hbm] * 7,
        out_specs=(vmem,) * 4,
        scratch_shapes=[
            pltpu.VMEM(block_map.shape, jnp.int32),
            pltpu.SMEM(block_map.shape, jnp.int32),
            pltpu.SMEM(context.shape, jnp.int32),
            pltpu.SMEM(gates.shape, jnp.float32),
            pltpu.VMEM((2, block_map.shape[1]), jnp.int32),
            pltpu.SMEM((2, block_map.shape[1]), jnp.int32),
            pltpu.VMEM((1, block), jnp.int32),
            pltpu.SMEM((1, block), jnp.int32),
            pltpu.VMEM((tokens, width), hidden.dtype),
            pltpu.VMEM(head.shape, head.dtype),
            pltpu.VMEM(tiles.shape, tiles.dtype),
            pltpu.VMEM((per + 1, tokens, block), teacher.dtype),
            pltpu.VMEM((n, tokens, block), teacher.dtype),
            pltpu.VMEM((n + 1, tokens, block), teacher.dtype),
            pltpu.VMEM((n, tokens, block), teacher.dtype),
            pltpu.VMEM((n, tokens, block), teacher.dtype),
            pltpu.VMEM((n + 1, tokens, block), jnp.float32),
            pltpu.VMEM((tokens, cols), jnp.float32),
            pltpu.VMEM((tokens, block), jnp.float32),
            pltpu.VMEM((levels, 2, tokens), jnp.float32),
            pltpu.VMEM((levels, 2, tokens), jnp.float32),
            pltpu.VMEM((2, tokens), jnp.float32),
            pltpu.VMEM((n, 2, tokens), jnp.float32),
            pltpu.SemaphoreType.DMA((8 + per,)),
            pltpu.SemaphoreType.DMA((CHUNKS,)),
            pltpu.SemaphoreType.DMA((n,)),
            pltpu.SemaphoreType.DMA((n,)),
            pltpu.SemaphoreType.DMA((levels,)),
            pltpu.SemaphoreType.DMA((levels,)),
            pltpu.SemaphoreType.DMA((levels,)),
            pltpu.SemaphoreType.DMA((levels,)),
            pltpu.SemaphoreType.DMA((n,)),
            pltpu.SemaphoreType.DMA((n,)),
        ],
        compiler_params=pltpu.CompilerParams(
            collective_id=0, has_side_effects=True, vmem_limit_bytes=48 << 20
        ),
        name="exchange",
    )(block_map, context, gates, hidden, head, teacher, tiles)


def gradient_kernel(
    inv_root,
    rows,
    cols_ref,
    scaled_ref,
    mapped_ref,
    turned_ref,
    grad_hbm,
    out_hbm,
    kl_ref,
    grad_ref,
    out_ref,
    grad_sem,
    out_sem,
):
    pieces, splits = out_sem.shape
    chunk = grad_ref.shape[1] // pieces
    span = out_ref.shape[0] // splits
    inverse = cols_ref[:, 0:1]

    def save_grad(c):
        part = pl.ds(pl.multiple_of(c * chunk, chunk), chunk)
        return pltpu.make_async_copy(grad_ref.at[:, part], grad_hbm.at[:, part], grad_sem.at[c])

    def save_out(c, r):
        part = pl.ds(pl.multiple_of(c * chunk, chunk), chunk)
        lines = pl.ds(r * span, span)
        return pltpu.make_async_copy(
            out_ref.at[lines, part], out_hbm.at[lines, part], out_sem.at[c, r]
        )

    def column(c, carry):
        part = pl.ds(pl.multiple_of(c * chunk, chunk), chunk)
        grad_ref[:, part] = (scaled_ref[:, part] - mapped_ref[:, part] * inverse).astype(
            grad_ref.dtype
        )
        for r in range(splits):
            lines = pl.ds(r * span, span)
            out_ref[lines, part] = (
                jnp.dot(turned_ref[lines, :], grad_ref[:, part], preferred_element_type=jnp.float32)
                * inv_root
            ).astype(out_ref.dtype)
            save_out(c, r).start()
        save_grad(c).start()
        return carry

    lax.fori_loop(0, pieces, column, 0)
    kl_ref[0, 0] = jnp.max(cols_ref[0:1, 1:2]) * (1.0 / rows)

    def drain(c, carry):
        for r in range(splits):
            save_out(c, r).wait()
        save_grad(c).wait()
        return carry

    lax.fori_loop(0, pieces, drain, 0)


def gradients(scaled, mapped, turned, cols, inv_root, rows):
    tokens, columns = scaled.shape
    width = turned.shape[0]
    hbm = pl.BlockSpec(memory_space=pl.ANY)
    vmem = pl.BlockSpec(memory_space=pltpu.VMEM)
    return pl.pallas_call(
        functools.partial(gradient_kernel, inv_root, rows),
        out_shape=(
            jax.ShapeDtypeStruct((tokens, columns), jnp.bfloat16),
            jax.ShapeDtypeStruct((width, columns), jnp.bfloat16),
            jax.ShapeDtypeStruct((1, 1), jnp.float32),
        ),
        in_specs=[vmem] * 4,
        out_specs=(hbm, hbm, pl.BlockSpec(memory_space=pltpu.SMEM)),
        scratch_shapes=[
            pltpu.VMEM((tokens, columns), jnp.bfloat16),
            pltpu.VMEM((width, columns), jnp.bfloat16),
            pltpu.SemaphoreType.DMA((PIECES,)),
            pltpu.SemaphoreType.DMA((PIECES, SPLITS)),
        ],
        compiler_params=pltpu.CompilerParams(vmem_limit_bytes=40 << 20),
        name="gradients",
    )(cols, scaled, mapped, turned)


def per_device(
    hidden_states, student_head, teacher_probs, block_map, context, map_gates, map_tiles
):
    voc_count = lax.axis_size("voc")
    rows_total = hidden_states.shape[0] * lax.axis_size("row")
    inv_root = 1.0 / math.sqrt(rows_total)
    vocab_total = student_head.shape[1] * voc_count
    blocks, fanout, block, _ = map_tiles.shape
    head = lax.all_gather(student_head, "row", axis=0, tiled=True)
    scaled, mapped, turned, cols = exchange(
        hidden_states,
        head,
        teacher_probs,
        block_map.T,
        context,
        map_gates.transpose(0, 2, 1),
        map_tiles.reshape(blocks * fanout, block, block),
        vocab_total,
    )
    grad_logits, head_part, kl = gradients(
        scaled, mapped, turned, cols, inv_root, rows_total
    )
    kl_loss = lax.psum(kl.reshape(()), "row")
    head_grad = lax.psum_scatter(head_part, "row", scatter_dimension=0, tiled=True)
    return (grad_logits, head_grad, kl_loss)


def solution(mesh):
    placed = (
        P("row", None),
        P("row", "voc"),
        P("row", "voc"),
        P(),
        P("row"),
        P(None, "voc", None),
        P("voc", None, None, None),
    )
    return jax.shard_map(
        per_device,
        mesh=mesh,
        in_specs=placed,
        out_specs=(P("row", "voc"), P("row", "voc"), P()),
        check_vma=False,
    )
```

```python
import functools
import math

import jax
import jax.numpy as jnp
from jax import lax
from jax.experimental import pallas as pl
from jax.experimental.pallas import tpu as pltpu
from jax.sharding import PartitionSpec as P

MESH = pl.DeviceIdType.MESH
CHUNKS = 8
PIECES = 4
SPLITS = 4


def exchange_kernel(
    n,
    vocab,
    map_hbm,
    context_hbm,
    gates_hbm,
    hidden_hbm,
    head_hbm,
    teacher_hbm,
    tiles_hbm,
    scaled_ref,
    mapped_ref,
    turned_ref,
    cols_ref,
    map_vec,
    map_ref,
    context_ref,
    gates_ref,
    take_vec,
    take_ref,
    slot_vec,
    slot_ref,
    hidden_ref,
    head_ref,
    tiles_ref,
    shelf,
    outgoing,
    incoming,
    extra,
    landing,
    products,
    logits_ref,
    sums_ref,
    norm_out,
    norm_in,
    stats_out,
    stats_in,
    local_sem,
    head_sem,
    send_sem,
    recv_sem,
    extra_send,
    extra_recv,
    norm_send,
    norm_recv,
    stat_send,
    stat_recv,
):
    me = lax.axis_index("voc")
    levels = n.bit_length() - 1
    bits = [(me // 2**b) % 2 for b in range(levels)]
    flips = [(1 - 2 * bits[b]) * 2**b for b in range(levels)]
    tokens, width = hidden_ref.shape
    entries, block, _ = tiles_ref.shape
    fanout = map_vec.shape[0]
    blocks = entries // fanout
    per = shelf.shape[0] - 1
    windows = context_ref.shape[0]
    chunk = scaled_ref.shape[1] // CHUNKS
    rows = width // CHUNKS
    stride = 1 << per.bit_length()

    def partner(d):
        return me + sum(flips[b] for b in range(levels) if (d >> b) & 1)

    def reverse(e):
        return sum(((e // 2**b) % 2) * 2 ** (levels - 1 - b) for b in range(levels))

    far = list(range(n // 2, n))
    near = [d for d in range(1, n // 2) if (d >> 1).bit_count() < 2]
    bent = [d for d in range(1, n // 2) if (d >> 1).bit_count() >= 2]
    order = near + far + bent
    load_map = pltpu.make_async_copy(map_hbm, map_vec, local_sem.at[0])
    load_ids = pltpu.make_async_copy(map_hbm, map_ref, local_sem.at[1])
    load_context = pltpu.make_async_copy(context_hbm, context_ref, local_sem.at[2])
    load_gates = pltpu.make_async_copy(gates_hbm, gates_ref, local_sem.at[3])
    load_hidden = pltpu.make_async_copy(hidden_hbm, hidden_ref, local_sem.at[4])
    load_tiles = pltpu.make_async_copy(tiles_hbm, tiles_ref, local_sem.at[5])
    move_take = pltpu.make_async_copy(take_vec, take_ref, local_sem.at[6])
    move_slot = pltpu.make_async_copy(slot_vec, slot_ref, local_sem.at[7])

    def load_shelf(i):
        return pltpu.make_async_copy(
            teacher_hbm.at[:, pl.ds(i * block, block)], shelf.at[i], local_sem.at[8 + i]
        )

    def load_head(c):
        part = pl.ds(pl.multiple_of(c * chunk, chunk), chunk)
        return pltpu.make_async_copy(head_hbm.at[:, part], head_ref.at[:, part], head_sem.at[c])

    def main_copy(d):
        return pltpu.make_async_remote_copy(
            src_ref=outgoing.at[partner(d)],
            dst_ref=incoming.at[me],
            send_sem=send_sem.at[d],
            recv_sem=recv_sem.at[d],
            device_id={"voc": partner(d)},
            device_id_type=MESH,
        )

    def main_recv(d):
        return pltpu.make_async_remote_copy(
            src_ref=outgoing.at[partner(d)],
            dst_ref=incoming.at[partner(d)],
            send_sem=send_sem.at[d],
            recv_sem=recv_sem.at[d],
            device_id={"voc": partner(d)},
            device_id_type=MESH,
        )

    def region(s):
        return sum(bits[b] * (n >> (b + 1)) for b in range(s))

    def extra_copy(s):
        half = n >> (s + 1)
        away = region(s) + (1 - bits[s]) * half
        return pltpu.make_async_remote_copy(
            src_ref=extra.at[pl.ds(away, half)],
            dst_ref=landing.at[pl.ds(n - 2 * half, half)],
            send_sem=extra_send.at[s],
            recv_sem=extra_recv.at[s],
            device_id={"voc": partner(1 << s)},
            device_id_type=MESH,
        )

    def extra_finish(s):
        half = n >> (s + 1)
        kept = region(s) + bits[s] * half
        extra_copy(s).wait()

        def add(i, carry):
            extra[kept + i] = extra[kept + i] + landing[n - 2 * half + i]
            return carry

        lax.fori_loop(0, half, add, 0)
        if s + 1 < levels:
            extra_copy(s + 1).start()
        else:
            incoming[n] = extra[region(levels)]

    def norm_copy(s):
        return pltpu.make_async_remote_copy(
            src_ref=norm_out.at[s],
            dst_ref=norm_in.at[s],
            send_sem=norm_send.at[s],
            recv_sem=norm_recv.at[s],
            device_id={"voc": partner(1 << s)},
            device_id_type=MESH,
        )

    def norm_merge(s):
        norm_copy(s).wait()
        mine, other = norm_out[s, 0:1, :], norm_in[s, 0:1, :]
        top = jnp.maximum(mine, other)
        merged = norm_out[s, 1:2, :] * jnp.exp(mine - top)
        merged = merged + norm_in[s, 1:2, :] * jnp.exp(other - top)
        return top, merged

    def norm_step(s):
        top, merged = norm_merge(s)
        norm_out[s + 1, 0:1, :] = top
        norm_out[s + 1, 1:2, :] = merged
        norm_copy(s + 1).start()

    def stat_copy(d, owner):
        return pltpu.make_async_remote_copy(
            src_ref=stats_out,
            dst_ref=stats_in.at[owner],
            send_sem=stat_send.at[d],
            recv_sem=stat_recv.at[d],
            device_id={"voc": partner(d)},
            device_id_type=MESH,
        )

    load_map.start()
    for i in range(per):
        load_shelf(i).start()
    barrier = pltpu.get_barrier_semaphore()
    for d in reversed(range(1, n)):
        pl.semaphore_signal(barrier, inc=1, device_id={"voc": partner(d)}, device_id_type=MESH)
    load_ids.start()
    load_context.start()
    load_gates.start()
    load_hidden.start()
    load_tiles.start()

    load_map.wait()
    listed = map_vec[...]
    count = listed.shape[1]
    place = lax.broadcasted_iota(jnp.int32, listed.shape, 0) * blocks + (
        lax.broadcasted_iota(jnp.int32, listed.shape, 1) % blocks
    )
    offset = listed - me * per
    owned = (offset >= 0) & (offset < per)
    key = place * stride + offset
    big = entries * stride
    first = jnp.min(jnp.where(owned, key, big), axis=0, keepdims=True)
    last = jnp.max(jnp.where(owned, key, -1), axis=0, keepdims=True)
    shift = 1
    while shift < blocks:
        first = jnp.minimum(first, pltpu.roll(first, count - shift, 1))
        last = jnp.maximum(last, pltpu.roll(last, count - shift, 1))
        shift *= 2
    take_vec[0:1, :] = first & (stride - 1)
    take_vec[1:2, :] = jnp.where(last > first, last & (stride - 1), per)
    move_take.start()
    shelf[per] = jnp.zeros(shelf.shape[1:], shelf.dtype)
    move_take.wait()
    for i in range(per):
        load_shelf(i).wait()

    def fill(e, carry):
        outgoing[e] = shelf[take_ref[0, e * blocks]]
        extra[reverse(e)] = shelf[take_ref[1, e * blocks]]
        return carry

    lax.fori_loop(0, n, fill, 0)
    pl.semaphore_wait(barrier, n - 1)
    extra_copy(0).start()
    for d in order:
        main_copy(d).start()
    incoming[me] = outgoing[me]
    for c in range(CHUNKS):
        load_head(c).start()

    load_ids.wait()
    lane = lax.broadcasted_iota(jnp.int32, (1, block), 1)
    low = lane * per
    own_first = jnp.full((1, block), entries, jnp.int32)
    own_second = jnp.full((1, block), -1, jnp.int32)
    for p in reversed(range(entries)):
        wanted = map_ref[p // blocks, me * blocks + p % blocks]
        hit = (wanted >= low) & (wanted < low + per) & (lane < n)
        own_second = jnp.where(hit & (own_first < entries), own_first, own_second)
        own_first = jnp.where(hit, p, own_first)
    doubled = jnp.max(own_second, axis=1, keepdims=True)
    chosen = jnp.where(lane == n, doubled, own_first)
    slot_vec[...] = jnp.where(chosen < entries, chosen, 0)
    move_slot.start()
    move_slot.wait()
    load_context.wait()
    load_gates.wait()
    load_hidden.wait()

    def column(c, carry):
        load_head(c).wait()
        part = pl.ds(pl.multiple_of(c * chunk, chunk), chunk)
        logits_ref[:, part] = jnp.dot(
            hidden_ref[...], head_ref[:, part], preferred_element_type=jnp.float32
        )
        return carry

    def turn(c, carry):
        span = pl.ds(pl.multiple_of(c * rows, rows), rows)
        turned_ref[span, :] = hidden_ref[:, span].T
        return carry

    def multiply(slot):
        place = slot_ref[0, slot]
        k = place // blocks
        b = place - k * blocks
        value = jnp.dot(
            incoming[slot], tiles_ref[b * fanout + k], preferred_element_type=jnp.float32
        )
        span = tokens // windows
        for w in range(windows):
            gate = gates_ref[context_ref[w], k, b]
            products[slot, w * span : (w + 1) * span] = value[w * span : (w + 1) * span] * gate

    def take(group):
        for d in group:
            main_recv(d).wait_recv()
        for d in group:
            multiply(partner(d))

    early = CHUNKS // 3
    lax.fori_loop(0, early, column, 0)
    extra_finish(0)
    lax.fori_loop(early, CHUNKS, column, 0)
    lanes = lax.broadcasted_iota(jnp.int32, (tokens, block), 1)
    peak = jnp.max(logits_ref[...], axis=1, keepdims=True)
    summed = jnp.sum(jnp.exp(logits_ref[...] - peak), axis=1, keepdims=True)
    norm_out[0] = jnp.where(lanes == 0, peak, summed).T[:2]
    norm_copy(0).start()
    lax.fori_loop(0, CHUNKS, turn, 0)
    load_tiles.wait()
    norm_step(0)
    multiply(me)
    for s in range(1, levels - 1):
        extra_finish(s)
        if s < levels - 2:
            norm_step(s)
        if s == levels - 3:
            take(near)
            norm_step(s + 1)
        if s == levels - 2:
            take(bent)
    top, merged = norm_merge(levels - 1)
    log_norm = top + jnp.log(merged)
    line = lax.broadcasted_iota(jnp.int32, (block, tokens), 0)
    cols_ref[...] = jnp.where(line == 0, log_norm, 0.0).T

    def scale(c, carry):
        part = pl.ds(pl.multiple_of(c * chunk, chunk), chunk)
        centred = logits_ref[:, part] - cols_ref[:, 0:1]
        logits_ref[:, part] = centred
        scaled_ref[:, part] = vocab * jnp.exp(centred)
        return carry

    lax.fori_loop(0, CHUNKS, scale, 0)
    extra_finish(levels - 1)
    multiply(n)
    quarter = len(far) // 2
    for i in range(0, len(far), quarter):
        take(far[i : i + quarter])

    slots = []
    for b in range(blocks):
        for k in range(fanout):
            source = map_ref[k, me * blocks + b] // per
            slots.append(jnp.where(slot_ref[0, source] == k * blocks + b, source, n))
    strip = tokens // CHUNKS

    def combine(i, carry):
        span = pl.ds(pl.multiple_of(i * strip, strip), strip)
        total = jnp.zeros((strip, block), jnp.float32)
        cross = jnp.zeros((strip, block), jnp.float32)
        for b in range(blocks):
            value = products[slots[b * fanout], span]
            for k in range(1, fanout):
                value = value + products[slots[b * fanout + k], span]
            part = slice(b * block, (b + 1) * block)
            mapped_ref[span, part] = value
            total = total + value
            cross = cross + value * (jnp.log(value) - logits_ref[span, part])
        sums_ref[0, span, :] = total
        sums_ref[1, span, :] = cross
        return carry

    lax.fori_loop(0, CHUNKS, combine, 0, unroll=2)
    for i in range(2):
        stats_out[i : i + 1, :] = jnp.sum(sums_ref[i].T, axis=0, keepdims=True)
    for d in reversed(range(1, n)):
        stat_copy(d, me).start()
    stats_in[me] = stats_out[...]
    for d in order:
        main_copy(d).wait_send()
    for d in reversed(range(1, n)):
        stat_copy(d, partner(d)).wait_recv()
    row_total = jnp.sum(stats_in[:, 0, :], axis=0, keepdims=True)
    crosses = jnp.sum(stats_in[:, 1, :], axis=0, keepdims=True)
    divergence = crosses / row_total - jnp.log(row_total)
    divergence = jnp.sum(divergence, axis=1, keepdims=True)
    cols_ref[...] = jnp.where(line == 0, vocab / row_total, divergence).T
    for d in order:
        stat_copy(d, me).wait_send()


def exchange(hidden, head, teacher, block_map, context, gates, tiles, vocab):
    n = lax.axis_size("voc")
    tokens, width = hidden.shape
    cols = head.shape[1]
    block = tiles.shape[-1]
    per = teacher.shape[1] // block
    levels = n.bit_length() - 1
    hbm = pl.BlockSpec(memory_space=pl.ANY)
    vmem = pl.BlockSpec(memory_space=pltpu.VMEM)
    return pl.pallas_call(
        functools.partial(exchange_kernel, n, float(vocab)),
        out_shape=(
            pltpu.VMEM((tokens, cols), jnp.float32),
            pltpu.VMEM((tokens, cols), jnp.float32),
            pltpu.VMEM((width, tokens), hidden.dtype),
            pltpu.VMEM((tokens, block), jnp.float32),
        ),
        in_specs=[hbm] * 7,
        out_specs=(vmem,) * 4,
        scratch_shapes=[
            pltpu.VMEM(block_map.shape, jnp.int32),
            pltpu.SMEM(block_map.shape, jnp.int32),
            pltpu.SMEM(context.shape, jnp.int32),
            pltpu.SMEM(gates.shape, jnp.float32),
            pltpu.VMEM((2, block_map.shape[1]), jnp.int32),
            pltpu.SMEM((2, block_map.shape[1]), jnp.int32),
            pltpu.VMEM((1, block), jnp.int32),
            pltpu.SMEM((1, block), jnp.int32),
            pltpu.VMEM((tokens, width), hidden.dtype),
            pltpu.VMEM(head.shape, head.dtype),
            pltpu.VMEM(tiles.shape, tiles.dtype),
            pltpu.VMEM((per + 1, tokens, block), teacher.dtype),
            pltpu.VMEM((n, tokens, block), teacher.dtype),
            pltpu.VMEM((n + 1, tokens, block), teacher.dtype),
            pltpu.VMEM((n, tokens, block), teacher.dtype),
            pltpu.VMEM((n, tokens, block), teacher.dtype),
            pltpu.VMEM((n + 1, tokens, block), jnp.float32),
            pltpu.VMEM((tokens, cols), jnp.float32),
            pltpu.VMEM((2, tokens, block), jnp.float32),
            pltpu.VMEM((levels, 2, tokens), jnp.float32),
            pltpu.VMEM((levels, 2, tokens), jnp.float32),
            pltpu.VMEM((2, tokens), jnp.float32),
            pltpu.VMEM((n, 2, tokens), jnp.float32),
            pltpu.SemaphoreType.DMA((8 + per,)),
            pltpu.SemaphoreType.DMA((CHUNKS,)),
            pltpu.SemaphoreType.DMA((n,)),
            pltpu.SemaphoreType.DMA((n,)),
            pltpu.SemaphoreType.DMA((levels,)),
            pltpu.SemaphoreType.DMA((levels,)),
            pltpu.SemaphoreType.DMA((levels,)),
            pltpu.SemaphoreType.DMA((levels,)),
            pltpu.SemaphoreType.DMA((n,)),
            pltpu.SemaphoreType.DMA((n,)),
        ],
        compiler_params=pltpu.CompilerParams(
            collective_id=0, has_side_effects=True, vmem_limit_bytes=48 << 20
        ),
        name="exchange",
    )(block_map, context, gates, hidden, head, teacher, tiles)


def gradient_kernel(
    inv_root,
    rows,
    cols_ref,
    scaled_ref,
    mapped_ref,
    turned_ref,
    grad_hbm,
    out_hbm,
    kl_ref,
    grad_ref,
    out_ref,
    grad_sem,
    out_sem,
):
    pieces, splits = out_sem.shape
    chunk = grad_ref.shape[1] // pieces
    span = out_ref.shape[0] // splits
    inverse = cols_ref[:, 0:1]

    def save_grad(c):
        part = pl.ds(pl.multiple_of(c * chunk, chunk), chunk)
        return pltpu.make_async_copy(grad_ref.at[:, part], grad_hbm.at[:, part], grad_sem.at[c])

    def save_out(c, r):
        part = pl.ds(pl.multiple_of(c * chunk, chunk), chunk)
        lines = pl.ds(r * span, span)
        return pltpu.make_async_copy(
            out_ref.at[lines, part], out_hbm.at[lines, part], out_sem.at[c, r]
        )

    def column(c, carry):
        part = pl.ds(pl.multiple_of(c * chunk, chunk), chunk)
        grad_ref[:, part] = (scaled_ref[:, part] - mapped_ref[:, part] * inverse).astype(
            grad_ref.dtype
        )
        for r in range(splits):
            lines = pl.ds(r * span, span)
            out_ref[lines, part] = (
                jnp.dot(turned_ref[lines, :], grad_ref[:, part], preferred_element_type=jnp.float32)
                * inv_root
            ).astype(out_ref.dtype)
            save_out(c, r).start()
        save_grad(c).start()
        return carry

    lax.fori_loop(0, pieces, column, 0)
    kl_ref[0, 0] = jnp.max(cols_ref[0:1, 1:2]) * (1.0 / rows)

    def drain(c, carry):
        for r in range(splits):
            save_out(c, r).wait()
        save_grad(c).wait()
        return carry

    lax.fori_loop(0, pieces, drain, 0)


def gradients(scaled, mapped, turned, cols, inv_root, rows):
    tokens, columns = scaled.shape
    width = turned.shape[0]
    hbm = pl.BlockSpec(memory_space=pl.ANY)
    vmem = pl.BlockSpec(memory_space=pltpu.VMEM)
    return pl.pallas_call(
        functools.partial(gradient_kernel, inv_root, rows),
        out_shape=(
            jax.ShapeDtypeStruct((tokens, columns), jnp.bfloat16),
            jax.ShapeDtypeStruct((width, columns), jnp.bfloat16),
            jax.ShapeDtypeStruct((1, 1), jnp.float32),
        ),
        in_specs=[vmem] * 4,
        out_specs=(hbm, hbm, pl.BlockSpec(memory_space=pltpu.SMEM)),
        scratch_shapes=[
            pltpu.VMEM((tokens, columns), jnp.bfloat16),
            pltpu.VMEM((width, columns), jnp.bfloat16),
            pltpu.SemaphoreType.DMA((PIECES,)),
            pltpu.SemaphoreType.DMA((PIECES, SPLITS)),
        ],
        compiler_params=pltpu.CompilerParams(vmem_limit_bytes=40 << 20),
        name="gradients",
    )(cols, scaled, mapped, turned)


def per_device(
    hidden_states, student_head, teacher_probs, block_map, context, map_gates, map_tiles
):
    voc_count = lax.axis_size("voc")
    rows_total = hidden_states.shape[0] * lax.axis_size("row")
    inv_root = 1.0 / math.sqrt(rows_total)
    vocab_total = student_head.shape[1] * voc_count
    blocks, fanout, block, _ = map_tiles.shape
    head = lax.all_gather(student_head, "row", axis=0, tiled=True)
    scaled, mapped, turned, cols = exchange(
        hidden_states,
        head,
        teacher_probs,
        block_map.T,
        context,
        map_gates.transpose(0, 2, 1),
        map_tiles.reshape(blocks * fanout, block, block),
        vocab_total,
    )
    grad_logits, head_part, kl = gradients(
        scaled, mapped, turned, cols, inv_root, rows_total
    )
    kl_loss = lax.psum(kl.reshape(()), "row")
    head_grad = lax.psum_scatter(head_part, "row", scatter_dimension=0, tiled=True)
    return (grad_logits, head_grad, kl_loss)


def solution(mesh):
    placed = (
        P("row", None),
        P("row", "voc"),
        P("row", "voc"),
        P(),
        P("row"),
        P(None, "voc", None),
        P("voc", None, None, None),
    )
    return jax.shard_map(
        per_device,
        mesh=mesh,
        in_specs=placed,
        out_specs=(P("row", "voc"), P("row", "voc"), P()),
        check_vma=False,
    )
```

```python
import functools
import math

import jax
import jax.numpy as jnp
from jax import lax
from jax.experimental import pallas as pl
from jax.experimental.pallas import tpu as pltpu
from jax.sharding import PartitionSpec as P

MESH = pl.DeviceIdType.MESH
CHUNKS = 8
PIECES = 4
SPLITS = 4


def exchange_kernel(
    n,
    vocab,
    map_hbm,
    context_hbm,
    gates_hbm,
    hidden_hbm,
    head_hbm,
    teacher_hbm,
    tiles_hbm,
    scaled_ref,
    mapped_ref,
    turned_ref,
    cols_ref,
    map_vec,
    map_ref,
    context_ref,
    gates_ref,
    take_vec,
    take_ref,
    slot_vec,
    slot_ref,
    hidden_ref,
    head_ref,
    tiles_ref,
    shelf,
    outgoing,
    incoming,
    extra,
    landing,
    products,
    logits_ref,
    sums_ref,
    norm_out,
    norm_in,
    stats_out,
    stats_in,
    local_sem,
    head_sem,
    send_sem,
    recv_sem,
    extra_send,
    extra_recv,
    norm_send,
    norm_recv,
    stat_send,
    stat_recv,
):
    me = lax.axis_index("voc")
    levels = n.bit_length() - 1
    bits = [(me // 2**b) % 2 for b in range(levels)]
    flips = [(1 - 2 * bits[b]) * 2**b for b in range(levels)]
    tokens, width = hidden_ref.shape
    entries, block, _ = tiles_ref.shape
    fanout = map_vec.shape[0]
    blocks = entries // fanout
    per = shelf.shape[0] - 1
    windows = context_ref.shape[0]
    chunk = scaled_ref.shape[1] // CHUNKS
    rows = width // CHUNKS
    stride = 1 << per.bit_length()

    def partner(d):
        return me + sum(flips[b] for b in range(levels) if (d >> b) & 1)

    def reverse(e):
        return sum(((e // 2**b) % 2) * 2 ** (levels - 1 - b) for b in range(levels))

    far = [d + h for d in range(n // 2, 3 * n // 4) for h in (0, n // 4)]
    near = [d for d in range(1, n // 2) if (d >> 1).bit_count() < 2]
    bent = [d for d in range(1, n // 2) if (d >> 1).bit_count() >= 2]
    order = near + far + bent
    load_map = pltpu.make_async_copy(map_hbm, map_vec, local_sem.at[0])
    load_ids = pltpu.make_async_copy(map_hbm, map_ref, local_sem.at[1])
    load_context = pltpu.make_async_copy(context_hbm, context_ref, local_sem.at[2])
    load_gates = pltpu.make_async_copy(gates_hbm, gates_ref, local_sem.at[3])
    load_hidden = pltpu.make_async_copy(hidden_hbm, hidden_ref, local_sem.at[4])
    load_tiles = pltpu.make_async_copy(tiles_hbm, tiles_ref, local_sem.at[5])
    move_take = pltpu.make_async_copy(take_vec, take_ref, local_sem.at[6])
    move_slot = pltpu.make_async_copy(slot_vec, slot_ref, local_sem.at[7])

    def load_shelf(i):
        return pltpu.make_async_copy(
            teacher_hbm.at[:, pl.ds(i * block, block)], shelf.at[i], local_sem.at[8 + i]
        )

    def load_head(c):
        part = pl.ds(pl.multiple_of(c * chunk, chunk), chunk)
        return pltpu.make_async_copy(head_hbm.at[:, part], head_ref.at[:, part], head_sem.at[c])

    def main_copy(d):
        return pltpu.make_async_remote_copy(
            src_ref=outgoing.at[partner(d)],
            dst_ref=incoming.at[me],
            send_sem=send_sem.at[d],
            recv_sem=recv_sem.at[d],
            device_id={"voc": partner(d)},
            device_id_type=MESH,
        )

    def main_recv(d):
        return pltpu.make_async_remote_copy(
            src_ref=outgoing.at[partner(d)],
            dst_ref=incoming.at[partner(d)],
            send_sem=send_sem.at[d],
            recv_sem=recv_sem.at[d],
            device_id={"voc": partner(d)},
            device_id_type=MESH,
        )

    def region(s):
        return sum(bits[b] * (n >> (b + 1)) for b in range(s))

    def extra_copy(s):
        half = n >> (s + 1)
        away = region(s) + (1 - bits[s]) * half
        return pltpu.make_async_remote_copy(
            src_ref=extra.at[pl.ds(away, half)],
            dst_ref=landing.at[pl.ds(n - 2 * half, half)],
            send_sem=extra_send.at[s],
            recv_sem=extra_recv.at[s],
            device_id={"voc": partner(1 << s)},
            device_id_type=MESH,
        )

    def extra_finish(s):
        half = n >> (s + 1)
        kept = region(s) + bits[s] * half
        extra_copy(s).wait()

        def add(i, carry):
            extra[kept + i] = extra[kept + i] + landing[n - 2 * half + i]
            return carry

        lax.fori_loop(0, half, add, 0)
        if s + 1 < levels:
            extra_copy(s + 1).start()
        else:
            incoming[n] = extra[region(levels)]

    def norm_copy(s):
        return pltpu.make_async_remote_copy(
            src_ref=norm_out.at[s],
            dst_ref=norm_in.at[s],
            send_sem=norm_send.at[s],
            recv_sem=norm_recv.at[s],
            device_id={"voc": partner(1 << s)},
            device_id_type=MESH,
        )

    def norm_merge(s):
        norm_copy(s).wait()
        mine, other = norm_out[s, 0:1, :], norm_in[s, 0:1, :]
        top = jnp.maximum(mine, other)
        merged = norm_out[s, 1:2, :] * jnp.exp(mine - top)
        merged = merged + norm_in[s, 1:2, :] * jnp.exp(other - top)
        return top, merged

    def norm_step(s):
        top, merged = norm_merge(s)
        norm_out[s + 1, 0:1, :] = top
        norm_out[s + 1, 1:2, :] = merged
        norm_copy(s + 1).start()

    def stat_copy(d, owner):
        return pltpu.make_async_remote_copy(
            src_ref=stats_out,
            dst_ref=stats_in.at[owner],
            send_sem=stat_send.at[d],
            recv_sem=stat_recv.at[d],
            device_id={"voc": partner(d)},
            device_id_type=MESH,
        )

    load_map.start()
    for i in range(per):
        load_shelf(i).start()
    barrier = pltpu.get_barrier_semaphore()
    for d in reversed(range(1, n)):
        pl.semaphore_signal(barrier, inc=1, device_id={"voc": partner(d)}, device_id_type=MESH)
    load_ids.start()
    load_context.start()
    load_gates.start()
    load_hidden.start()
    load_tiles.start()

    load_map.wait()
    listed = map_vec[...]
    count = listed.shape[1]
    place = lax.broadcasted_iota(jnp.int32, listed.shape, 0) * blocks + (
        lax.broadcasted_iota(jnp.int32, listed.shape, 1) % blocks
    )
    offset = listed - me * per
    owned = (offset >= 0) & (offset < per)
    key = place * stride + offset
    big = entries * stride
    first = jnp.min(jnp.where(owned, key, big), axis=0, keepdims=True)
    last = jnp.max(jnp.where(owned, key, -1), axis=0, keepdims=True)
    shift = 1
    while shift < blocks:
        first = jnp.minimum(first, pltpu.roll(first, count - shift, 1))
        last = jnp.maximum(last, pltpu.roll(last, count - shift, 1))
        shift *= 2
    take_vec[0:1, :] = first & (stride - 1)
    take_vec[1:2, :] = jnp.where(last > first, last & (stride - 1), per)
    move_take.start()
    shelf[per] = jnp.zeros(shelf.shape[1:], shelf.dtype)
    move_take.wait()
    for i in range(per):
        load_shelf(i).wait()

    def fill(e, carry):
        outgoing[e] = shelf[take_ref[0, e * blocks]]
        extra[reverse(e)] = shelf[take_ref[1, e * blocks]]
        return carry

    lax.fori_loop(0, n, fill, 0)
    pl.semaphore_wait(barrier, n - 1)
    extra_copy(0).start()
    for d in order:
        main_copy(d).start()
    incoming[me] = outgoing[me]
    for c in range(CHUNKS):
        load_head(c).start()

    load_ids.wait()
    lane = lax.broadcasted_iota(jnp.int32, (1, block), 1)
    low = lane * per
    own_first = jnp.full((1, block), entries, jnp.int32)
    own_second = jnp.full((1, block), -1, jnp.int32)
    for p in reversed(range(entries)):
        wanted = map_ref[p // blocks, me * blocks + p % blocks]
        hit = (wanted >= low) & (wanted < low + per) & (lane < n)
        own_second = jnp.where(hit & (own_first < entries), own_first, own_second)
        own_first = jnp.where(hit, p, own_first)
    doubled = jnp.max(own_second, axis=1, keepdims=True)
    chosen = jnp.where(lane == n, doubled, own_first)
    slot_vec[...] = jnp.where(chosen < entries, chosen, 0)
    move_slot.start()
    move_slot.wait()
    load_context.wait()
    load_gates.wait()
    load_hidden.wait()

    def column(c, carry):
        load_head(c).wait()
        part = pl.ds(pl.multiple_of(c * chunk, chunk), chunk)
        logits_ref[:, part] = jnp.dot(
            hidden_ref[...], head_ref[:, part], preferred_element_type=jnp.float32
        )
        return carry

    def turn(c, carry):
        span = pl.ds(pl.multiple_of(c * rows, rows), rows)
        turned_ref[span, :] = hidden_ref[:, span].T
        return carry

    def multiply(slot):
        place = slot_ref[0, slot]
        k = place // blocks
        b = place - k * blocks
        value = jnp.dot(
            incoming[slot], tiles_ref[b * fanout + k], preferred_element_type=jnp.float32
        )
        span = tokens // windows
        for w in range(windows):
            gate = gates_ref[context_ref[w], k, b]
            products[slot, w * span : (w + 1) * span] = value[w * span : (w + 1) * span] * gate

    def take(group):
        for d in group:
            main_recv(d).wait_recv()
        for d in group:
            multiply(partner(d))

    early = CHUNKS // 3
    lax.fori_loop(0, early, column, 0)
    extra_finish(0)
    lax.fori_loop(early, CHUNKS, column, 0)
    lanes = lax.broadcasted_iota(jnp.int32, (tokens, block), 1)
    peak = jnp.max(logits_ref[...], axis=1, keepdims=True)
    summed = jnp.sum(jnp.exp(logits_ref[...] - peak), axis=1, keepdims=True)
    norm_out[0] = jnp.where(lanes == 0, peak, summed).T[:2]
    norm_copy(0).start()
    lax.fori_loop(0, CHUNKS, turn, 0)
    load_tiles.wait()
    norm_step(0)
    multiply(me)
    for s in range(1, levels - 1):
        extra_finish(s)
        if s < levels - 2:
            norm_step(s)
        if s == levels - 3:
            take(near)
            norm_step(s + 1)
        if s == levels - 2:
            take(bent)
    top, merged = norm_merge(levels - 1)
    log_norm = top + jnp.log(merged)
    line = lax.broadcasted_iota(jnp.int32, (block, tokens), 0)
    cols_ref[...] = jnp.where(line == 0, log_norm, 0.0).T

    def scale(c, carry):
        part = pl.ds(pl.multiple_of(c * chunk, chunk), chunk)
        centred = logits_ref[:, part] - cols_ref[:, 0:1]
        logits_ref[:, part] = centred
        scaled_ref[:, part] = vocab * jnp.exp(centred)
        return carry

    lax.fori_loop(0, CHUNKS, scale, 0)
    extra_finish(levels - 1)
    multiply(n)
    quarter = len(far) // 2
    for i in range(0, len(far), quarter):
        take(far[i : i + quarter])

    slots = []
    for b in range(blocks):
        for k in range(fanout):
            source = map_ref[k, me * blocks + b] // per
            slots.append(jnp.where(slot_ref[0, source] == k * blocks + b, source, n))
    strip = tokens // CHUNKS

    def combine(i, carry):
        span = pl.ds(pl.multiple_of(i * strip, strip), strip)
        total = jnp.zeros((strip, block), jnp.float32)
        cross = jnp.zeros((strip, block), jnp.float32)
        for b in range(blocks):
            value = products[slots[b * fanout], span]
            for k in range(1, fanout):
                value = value + products[slots[b * fanout + k], span]
            part = slice(b * block, (b + 1) * block)
            mapped_ref[span, part] = value
            total = total + value
            cross = cross + value * (jnp.log(value) - logits_ref[span, part])
        sums_ref[0, span, :] = total
        sums_ref[1, span, :] = cross
        return carry

    lax.fori_loop(0, CHUNKS, combine, 0, unroll=2)
    for i in range(2):
        stats_out[i : i + 1, :] = jnp.sum(sums_ref[i].T, axis=0, keepdims=True)
    for d in reversed(range(1, n)):
        stat_copy(d, me).start()
    stats_in[me] = stats_out[...]
    for d in order:
        main_copy(d).wait_send()
    for d in reversed(range(1, n)):
        stat_copy(d, partner(d)).wait_recv()
    row_total = jnp.sum(stats_in[:, 0, :], axis=0, keepdims=True)
    crosses = jnp.sum(stats_in[:, 1, :], axis=0, keepdims=True)
    divergence = crosses / row_total - jnp.log(row_total)
    divergence = jnp.sum(divergence, axis=1, keepdims=True)
    cols_ref[...] = jnp.where(line == 0, vocab / row_total, divergence).T
    for d in order:
        stat_copy(d, me).wait_send()


def exchange(hidden, head, teacher, block_map, context, gates, tiles, vocab):
    n = lax.axis_size("voc")
    tokens, width = hidden.shape
    cols = head.shape[1]
    block = tiles.shape[-1]
    per = teacher.shape[1] // block
    levels = n.bit_length() - 1
    hbm = pl.BlockSpec(memory_space=pl.ANY)
    vmem = pl.BlockSpec(memory_space=pltpu.VMEM)
    return pl.pallas_call(
        functools.partial(exchange_kernel, n, float(vocab)),
        out_shape=(
            pltpu.VMEM((tokens, cols), jnp.float32),
            pltpu.VMEM((tokens, cols), jnp.float32),
            pltpu.VMEM((width, tokens), hidden.dtype),
            pltpu.VMEM((tokens, block), jnp.float32),
        ),
        in_specs=[hbm] * 7,
        out_specs=(vmem,) * 4,
        scratch_shapes=[
            pltpu.VMEM(block_map.shape, jnp.int32),
            pltpu.SMEM(block_map.shape, jnp.int32),
            pltpu.SMEM(context.shape, jnp.int32),
            pltpu.SMEM(gates.shape, jnp.float32),
            pltpu.VMEM((2, block_map.shape[1]), jnp.int32),
            pltpu.SMEM((2, block_map.shape[1]), jnp.int32),
            pltpu.VMEM((1, block), jnp.int32),
            pltpu.SMEM((1, block), jnp.int32),
            pltpu.VMEM((tokens, width), hidden.dtype),
            pltpu.VMEM(head.shape, head.dtype),
            pltpu.VMEM(tiles.shape, tiles.dtype),
            pltpu.VMEM((per + 1, tokens, block), teacher.dtype),
            pltpu.VMEM((n, tokens, block), teacher.dtype),
            pltpu.VMEM((n + 1, tokens, block), teacher.dtype),
            pltpu.VMEM((n, tokens, block), teacher.dtype),
            pltpu.VMEM((n, tokens, block), teacher.dtype),
            pltpu.VMEM((n + 1, tokens, block), jnp.float32),
            pltpu.VMEM((tokens, cols), jnp.float32),
            pltpu.VMEM((2, tokens, block), jnp.float32),
            pltpu.VMEM((levels, 2, tokens), jnp.float32),
            pltpu.VMEM((levels, 2, tokens), jnp.float32),
            pltpu.VMEM((2, tokens), jnp.float32),
            pltpu.VMEM((n, 2, tokens), jnp.float32),
            pltpu.SemaphoreType.DMA((8 + per,)),
            pltpu.SemaphoreType.DMA((CHUNKS,)),
            pltpu.SemaphoreType.DMA((n,)),
            pltpu.SemaphoreType.DMA((n,)),
            pltpu.SemaphoreType.DMA((levels,)),
            pltpu.SemaphoreType.DMA((levels,)),
            pltpu.SemaphoreType.DMA((levels,)),
            pltpu.SemaphoreType.DMA((levels,)),
            pltpu.SemaphoreType.DMA((n,)),
            pltpu.SemaphoreType.DMA((n,)),
        ],
        compiler_params=pltpu.CompilerParams(
            collective_id=0, has_side_effects=True, vmem_limit_bytes=48 << 20
        ),
        name="exchange",
    )(block_map, context, gates, hidden, head, teacher, tiles)


def gradient_kernel(
    inv_root,
    rows,
    cols_ref,
    scaled_ref,
    mapped_ref,
    turned_ref,
    grad_hbm,
    out_hbm,
    kl_ref,
    grad_ref,
    out_ref,
    grad_sem,
    out_sem,
):
    pieces, splits = out_sem.shape
    chunk = grad_ref.shape[1] // pieces
    span = out_ref.shape[0] // splits
    inverse = cols_ref[:, 0:1]

    def save_grad(c):
        part = pl.ds(pl.multiple_of(c * chunk, chunk), chunk)
        return pltpu.make_async_copy(grad_ref.at[:, part], grad_hbm.at[:, part], grad_sem.at[c])

    def save_out(c, r):
        part = pl.ds(pl.multiple_of(c * chunk, chunk), chunk)
        lines = pl.ds(r * span, span)
        return pltpu.make_async_copy(
            out_ref.at[lines, part], out_hbm.at[lines, part], out_sem.at[c, r]
        )

    def column(c, carry):
        part = pl.ds(pl.multiple_of(c * chunk, chunk), chunk)
        grad_ref[:, part] = (scaled_ref[:, part] - mapped_ref[:, part] * inverse).astype(
            grad_ref.dtype
        )
        for r in range(splits):
            lines = pl.ds(r * span, span)
            out_ref[lines, part] = (
                jnp.dot(turned_ref[lines, :], grad_ref[:, part], preferred_element_type=jnp.float32)
                * inv_root
            ).astype(out_ref.dtype)
            save_out(c, r).start()
        save_grad(c).start()
        return carry

    lax.fori_loop(0, pieces, column, 0)
    kl_ref[0, 0] = jnp.max(cols_ref[0:1, 1:2]) * (1.0 / rows)

    def drain(c, carry):
        for r in range(splits):
            save_out(c, r).wait()
        save_grad(c).wait()
        return carry

    lax.fori_loop(0, pieces, drain, 0)


def gradients(scaled, mapped, turned, cols, inv_root, rows):
    tokens, columns = scaled.shape
    width = turned.shape[0]
    hbm = pl.BlockSpec(memory_space=pl.ANY)
    vmem = pl.BlockSpec(memory_space=pltpu.VMEM)
    return pl.pallas_call(
        functools.partial(gradient_kernel, inv_root, rows),
        out_shape=(
            jax.ShapeDtypeStruct((tokens, columns), jnp.bfloat16),
            jax.ShapeDtypeStruct((width, columns), jnp.bfloat16),
            jax.ShapeDtypeStruct((1, 1), jnp.float32),
        ),
        in_specs=[vmem] * 4,
        out_specs=(hbm, hbm, pl.BlockSpec(memory_space=pltpu.SMEM)),
        scratch_shapes=[
            pltpu.VMEM((tokens, columns), jnp.bfloat16),
            pltpu.VMEM((width, columns), jnp.bfloat16),
            pltpu.SemaphoreType.DMA((PIECES,)),
            pltpu.SemaphoreType.DMA((PIECES, SPLITS)),
        ],
        compiler_params=pltpu.CompilerParams(vmem_limit_bytes=40 << 20),
        name="gradients",
    )(cols, scaled, mapped, turned)


def per_device(
    hidden_states, student_head, teacher_probs, block_map, context, map_gates, map_tiles
):
    voc_count = lax.axis_size("voc")
    rows_total = hidden_states.shape[0] * lax.axis_size("row")
    inv_root = 1.0 / math.sqrt(rows_total)
    vocab_total = student_head.shape[1] * voc_count
    blocks, fanout, block, _ = map_tiles.shape
    head = lax.all_gather(student_head, "row", axis=0, tiled=True)
    scaled, mapped, turned, cols = exchange(
        hidden_states,
        head,
        teacher_probs,
        block_map.T,
        context,
        map_gates.transpose(0, 2, 1),
        map_tiles.reshape(blocks * fanout, block, block),
        vocab_total,
    )
    grad_logits, head_part, kl = gradients(
        scaled, mapped, turned, cols, inv_root, rows_total
    )
    kl_loss = lax.psum(kl.reshape(()), "row")
    head_grad = lax.psum_scatter(head_part, "row", scatter_dimension=0, tiled=True)
    return (grad_logits, head_grad, kl_loss)


def solution(mesh):
    placed = (
        P("row", None),
        P("row", "voc"),
        P("row", "voc"),
        P(),
        P("row"),
        P(None, "voc", None),
        P("voc", None, None, None),
    )
    return jax.shard_map(
        per_device,
        mesh=mesh,
        in_specs=placed,
        out_specs=(P("row", "voc"), P("row", "voc"), P()),
        check_vma=False,
    )
```

```python
import functools
import math

import jax
import jax.numpy as jnp
from jax import lax
from jax.experimental import pallas as pl
from jax.experimental.pallas import tpu as pltpu
from jax.sharding import PartitionSpec as P

MESH = pl.DeviceIdType.MESH
CHUNKS = 8
PIECES = 4
SPLITS = 8


def exchange_kernel(
    n,
    vocab,
    map_hbm,
    context_hbm,
    gates_hbm,
    hidden_hbm,
    head_hbm,
    teacher_hbm,
    tiles_hbm,
    scaled_ref,
    mapped_ref,
    turned_ref,
    cols_ref,
    map_vec,
    map_ref,
    context_ref,
    gates_ref,
    take_vec,
    take_ref,
    slot_vec,
    slot_ref,
    hidden_ref,
    head_ref,
    tiles_ref,
    shelf,
    outgoing,
    incoming,
    extra,
    landing,
    products,
    logits_ref,
    sums_ref,
    norm_out,
    norm_in,
    stats_out,
    stats_in,
    local_sem,
    head_sem,
    send_sem,
    recv_sem,
    extra_send,
    extra_recv,
    norm_send,
    norm_recv,
    stat_send,
    stat_recv,
):
    me = lax.axis_index("voc")
    levels = n.bit_length() - 1
    bits = [(me // 2**b) % 2 for b in range(levels)]
    flips = [(1 - 2 * bits[b]) * 2**b for b in range(levels)]
    tokens, width = hidden_ref.shape
    entries, block, _ = tiles_ref.shape
    fanout = map_vec.shape[0]
    blocks = entries // fanout
    per = shelf.shape[0] - 1
    windows = context_ref.shape[0]
    chunk = scaled_ref.shape[1] // CHUNKS
    rows = width // CHUNKS
    stride = 1 << per.bit_length()

    def partner(d):
        return me + sum(flips[b] for b in range(levels) if (d >> b) & 1)

    def reverse(e):
        return sum(((e // 2**b) % 2) * 2 ** (levels - 1 - b) for b in range(levels))

    far = [d + h for d in range(n // 2, 3 * n // 4) for h in (0, n // 4)]
    near = [d for d in range(1, n // 2) if (d >> 1).bit_count() < 2]
    bent = [d for d in range(1, n // 2) if (d >> 1).bit_count() >= 2]
    order = near + far + bent
    load_map = pltpu.make_async_copy(map_hbm, map_vec, local_sem.at[0])
    load_ids = pltpu.make_async_copy(map_hbm, map_ref, local_sem.at[1])
    load_context = pltpu.make_async_copy(context_hbm, context_ref, local_sem.at[2])
    load_gates = pltpu.make_async_copy(gates_hbm, gates_ref, local_sem.at[3])
    load_hidden = pltpu.make_async_copy(hidden_hbm, hidden_ref, local_sem.at[4])
    load_tiles = pltpu.make_async_copy(tiles_hbm, tiles_ref, local_sem.at[5])
    move_take = pltpu.make_async_copy(take_vec, take_ref, local_sem.at[6])
    move_slot = pltpu.make_async_copy(slot_vec, slot_ref, local_sem.at[7])

    def load_shelf(i):
        return pltpu.make_async_copy(
            teacher_hbm.at[:, pl.ds(i * block, block)], shelf.at[i], local_sem.at[8 + i]
        )

    def load_head(c):
        part = pl.ds(pl.multiple_of(c * chunk, chunk), chunk)
        return pltpu.make_async_copy(head_hbm.at[:, part], head_ref.at[:, part], head_sem.at[c])

    def main_copy(d):
        return pltpu.make_async_remote_copy(
            src_ref=outgoing.at[partner(d)],
            dst_ref=incoming.at[me],
            send_sem=send_sem.at[0],
            recv_sem=recv_sem.at[d],
            device_id={"voc": partner(d)},
            device_id_type=MESH,
        )

    def sent_all(source, target, sent, received):
        return pltpu.make_async_remote_copy(
            src_ref=source,
            dst_ref=target,
            send_sem=sent,
            recv_sem=received,
            device_id={"voc": partner(1)},
            device_id_type=MESH,
        )

    def main_recv(d):
        return pltpu.make_async_remote_copy(
            src_ref=outgoing.at[partner(d)],
            dst_ref=incoming.at[partner(d)],
            send_sem=send_sem.at[0],
            recv_sem=recv_sem.at[d],
            device_id={"voc": partner(d)},
            device_id_type=MESH,
        )

    def region(s):
        return sum(bits[b] * (n >> (b + 1)) for b in range(s))

    def extra_copy(s):
        half = n >> (s + 1)
        away = region(s) + (1 - bits[s]) * half
        return pltpu.make_async_remote_copy(
            src_ref=extra.at[pl.ds(away, half)],
            dst_ref=landing.at[pl.ds(n - 2 * half, half)],
            send_sem=extra_send.at[s],
            recv_sem=extra_recv.at[s],
            device_id={"voc": partner(1 << s)},
            device_id_type=MESH,
        )

    def extra_finish(s):
        half = n >> (s + 1)
        kept = region(s) + bits[s] * half
        extra_copy(s).wait()

        def add(i, carry):
            extra[kept + i] = extra[kept + i] + landing[n - 2 * half + i]
            return carry

        lax.fori_loop(0, half, add, 0)
        if s + 1 < levels:
            extra_copy(s + 1).start()
        else:
            incoming[n] = extra[region(levels)]

    def norm_copy(s):
        return pltpu.make_async_remote_copy(
            src_ref=norm_out.at[s],
            dst_ref=norm_in.at[s],
            send_sem=norm_send.at[s],
            recv_sem=norm_recv.at[s],
            device_id={"voc": partner(1 << s)},
            device_id_type=MESH,
        )

    def norm_merge(s):
        norm_copy(s).wait()
        mine, other = norm_out[s, 0:1, :], norm_in[s, 0:1, :]
        top = jnp.maximum(mine, other)
        merged = norm_out[s, 1:2, :] * jnp.exp(mine - top)
        merged = merged + norm_in[s, 1:2, :] * jnp.exp(other - top)
        return top, merged

    def norm_step(s):
        top, merged = norm_merge(s)
        norm_out[s + 1, 0:1, :] = top
        norm_out[s + 1, 1:2, :] = merged
        norm_copy(s + 1).start()

    def stat_copy(d, owner):
        return pltpu.make_async_remote_copy(
            src_ref=stats_out,
            dst_ref=stats_in.at[owner],
            send_sem=stat_send.at[0],
            recv_sem=stat_recv.at[d],
            device_id={"voc": partner(d)},
            device_id_type=MESH,
        )

    load_map.start()
    for i in range(per):
        load_shelf(i).start()
    barrier = pltpu.get_barrier_semaphore()
    for d in reversed(range(1, n)):
        pl.semaphore_signal(barrier, inc=1, device_id={"voc": partner(d)}, device_id_type=MESH)
    load_ids.start()
    load_context.start()
    load_gates.start()
    load_hidden.start()
    load_tiles.start()

    load_map.wait()
    listed = map_vec[...]
    count = listed.shape[1]
    place = lax.broadcasted_iota(jnp.int32, listed.shape, 0) * blocks + (
        lax.broadcasted_iota(jnp.int32, listed.shape, 1) % blocks
    )
    offset = listed - me * per
    owned = (offset >= 0) & (offset < per)
    key = place * stride + offset
    big = entries * stride
    first = jnp.min(jnp.where(owned, key, big), axis=0, keepdims=True)
    last = jnp.max(jnp.where(owned, key, -1), axis=0, keepdims=True)
    shift = 1
    while shift < blocks:
        first = jnp.minimum(first, pltpu.roll(first, count - shift, 1))
        last = jnp.maximum(last, pltpu.roll(last, count - shift, 1))
        shift *= 2
    take_vec[0:1, :] = first & (stride - 1)
    take_vec[1:2, :] = jnp.where(last > first, last & (stride - 1), per)
    move_take.start()
    shelf[per] = jnp.zeros(shelf.shape[1:], shelf.dtype)
    move_take.wait()
    for i in range(per):
        load_shelf(i).wait()

    def fill(e, carry):
        outgoing[e] = shelf[take_ref[0, e * blocks]]
        extra[reverse(e)] = shelf[take_ref[1, e * blocks]]
        return carry

    lax.fori_loop(0, n, fill, 0)
    pl.semaphore_wait(barrier, n - 1)
    extra_copy(0).start()
    for d in order:
        main_copy(d).start()
    incoming[me] = outgoing[me]
    for c in range(CHUNKS):
        load_head(c).start()

    load_ids.wait()
    lane = lax.broadcasted_iota(jnp.int32, (1, block), 1)
    low = lane * per
    own_first = jnp.full((1, block), entries, jnp.int32)
    own_second = jnp.full((1, block), -1, jnp.int32)
    for p in reversed(range(entries)):
        wanted = map_ref[p // blocks, me * blocks + p % blocks]
        hit = (wanted >= low) & (wanted < low + per) & (lane < n)
        own_second = jnp.where(hit & (own_first < entries), own_first, own_second)
        own_first = jnp.where(hit, p, own_first)
    doubled = jnp.max(own_second, axis=1, keepdims=True)
    chosen = jnp.where(lane == n, doubled, own_first)
    slot_vec[...] = jnp.where(chosen < entries, chosen, 0)
    move_slot.start()
    move_slot.wait()
    load_context.wait()
    load_gates.wait()
    load_hidden.wait()

    def column(c, carry):
        load_head(c).wait()
        part = pl.ds(pl.multiple_of(c * chunk, chunk), chunk)
        logits_ref[:, part] = jnp.dot(
            hidden_ref[...], head_ref[:, part], preferred_element_type=jnp.float32
        )
        return carry

    def turn(c, carry):
        span = pl.ds(pl.multiple_of(c * rows, rows), rows)
        turned_ref[span, :] = hidden_ref[:, span].T
        return carry

    def multiply(slot):
        place = slot_ref[0, slot]
        k = place // blocks
        b = place - k * blocks
        value = jnp.dot(
            incoming[slot], tiles_ref[b * fanout + k], preferred_element_type=jnp.float32
        )
        span = tokens // windows
        for w in range(windows):
            gate = gates_ref[context_ref[w], k, b]
            products[slot, w * span : (w + 1) * span] = value[w * span : (w + 1) * span] * gate

    def take(group):
        for d in group:
            main_recv(d).wait_recv()
        for d in group:
            multiply(partner(d))

    early = CHUNKS // 3
    lax.fori_loop(0, early, column, 0)
    extra_finish(0)
    lax.fori_loop(early, CHUNKS, column, 0)
    lanes = lax.broadcasted_iota(jnp.int32, (tokens, block), 1)
    peak = jnp.max(logits_ref[...], axis=1, keepdims=True)
    summed = jnp.sum(jnp.exp(logits_ref[...] - peak), axis=1, keepdims=True)
    norm_out[0] = jnp.where(lanes == 0, peak, summed).T[:2]
    norm_copy(0).start()
    lax.fori_loop(0, CHUNKS, turn, 0)
    load_tiles.wait()
    norm_step(0)
    multiply(me)
    for s in range(1, levels - 1):
        extra_finish(s)
        if s < levels - 2:
            norm_step(s)
        if s == levels - 3:
            take(near)
            norm_step(s + 1)
        if s == levels - 2:
            take(bent)
    top, merged = norm_merge(levels - 1)
    log_norm = top + jnp.log(merged)
    line = lax.broadcasted_iota(jnp.int32, (block, tokens), 0)
    cols_ref[...] = jnp.where(line == 0, log_norm, 0.0).T

    def scale(c, carry):
        part = pl.ds(pl.multiple_of(c * chunk, chunk), chunk)
        centred = logits_ref[:, part] - cols_ref[:, 0:1]
        logits_ref[:, part] = centred
        scaled_ref[:, part] = vocab * jnp.exp(centred)
        return carry

    lax.fori_loop(0, CHUNKS, scale, 0)
    extra_finish(levels - 1)
    multiply(n)
    quarter = len(far) // 2
    for i in range(0, len(far), quarter):
        take(far[i : i + quarter])

    slots = []
    for b in range(blocks):
        for k in range(fanout):
            source = map_ref[k, me * blocks + b] // per
            slots.append(jnp.where(slot_ref[0, source] == k * blocks + b, source, n))
    strip = tokens // CHUNKS

    def combine(i, carry):
        span = pl.ds(pl.multiple_of(i * strip, strip), strip)
        total = jnp.zeros((strip, block), jnp.float32)
        cross = jnp.zeros((strip, block), jnp.float32)
        for b in range(blocks):
            value = products[slots[b * fanout], span]
            for k in range(1, fanout):
                value = value + products[slots[b * fanout + k], span]
            part = slice(b * block, (b + 1) * block)
            mapped_ref[span, part] = value
            total = total + value
            cross = cross + value * (jnp.log(value) - logits_ref[span, part])
        sums_ref[0, span, :] = total
        sums_ref[1, span, :] = cross
        return carry

    lax.fori_loop(0, CHUNKS, combine, 0, unroll=2)
    for i in range(2):
        stats_out[i : i + 1, :] = jnp.sum(sums_ref[i].T, axis=0, keepdims=True)
    for d in reversed(range(1, n)):
        stat_copy(d, me).start()
    stats_in[me] = stats_out[...]
    sent_all(outgoing.at[pl.ds(0, n - 1)], incoming.at[pl.ds(0, n - 1)], send_sem.at[0], recv_sem.at[0]).wait_send()
    for d in reversed(range(1, n)):
        stat_copy(d, partner(d)).wait_recv()
    sums = jnp.sum(stats_in[...], axis=0)
    row_total, crosses = sums[0:1], sums[1:2]
    divergence = crosses / row_total - jnp.log(row_total)
    divergence = jnp.sum(divergence, axis=1, keepdims=True)
    cols_ref[...] = jnp.where(line == 0, vocab / row_total, divergence).T
    both = stats_in.at[pl.ds(0, n - 1)]
    sent_all(both, both, stat_send.at[0], stat_recv.at[0]).wait_send()


def exchange(hidden, head, teacher, block_map, context, gates, tiles, vocab):
    n = lax.axis_size("voc")
    tokens, width = hidden.shape
    cols = head.shape[1]
    block = tiles.shape[-1]
    per = teacher.shape[1] // block
    levels = n.bit_length() - 1
    hbm = pl.BlockSpec(memory_space=pl.ANY)
    vmem = pl.BlockSpec(memory_space=pltpu.VMEM)
    return pl.pallas_call(
        functools.partial(exchange_kernel, n, float(vocab)),
        out_shape=(
            pltpu.VMEM((tokens, cols), jnp.float32),
            pltpu.VMEM((tokens, cols), jnp.float32),
            pltpu.VMEM((width, tokens), hidden.dtype),
            pltpu.VMEM((tokens, block), jnp.float32),
        ),
        in_specs=[hbm] * 7,
        out_specs=(vmem,) * 4,
        scratch_shapes=[
            pltpu.VMEM(block_map.shape, jnp.int32),
            pltpu.SMEM(block_map.shape, jnp.int32),
            pltpu.SMEM(context.shape, jnp.int32),
            pltpu.SMEM(gates.shape, jnp.float32),
            pltpu.VMEM((2, block_map.shape[1]), jnp.int32),
            pltpu.SMEM((2, block_map.shape[1]), jnp.int32),
            pltpu.VMEM((1, block), jnp.int32),
            pltpu.SMEM((1, block), jnp.int32),
            pltpu.VMEM((tokens, width), hidden.dtype),
            pltpu.VMEM(head.shape, head.dtype),
            pltpu.VMEM(tiles.shape, tiles.dtype),
            pltpu.VMEM((per + 1, tokens, block), teacher.dtype),
            pltpu.VMEM((n, tokens, block), teacher.dtype),
            pltpu.VMEM((n + 1, tokens, block), teacher.dtype),
            pltpu.VMEM((n, tokens, block), teacher.dtype),
            pltpu.VMEM((n, tokens, block), teacher.dtype),
            pltpu.VMEM((n + 1, tokens, block), jnp.float32),
            pltpu.VMEM((tokens, cols), jnp.float32),
            pltpu.VMEM((2, tokens, block), jnp.float32),
            pltpu.VMEM((levels, 2, tokens), jnp.float32),
            pltpu.VMEM((levels, 2, tokens), jnp.float32),
            pltpu.VMEM((2, tokens), jnp.float32),
            pltpu.VMEM((n, 2, tokens), jnp.float32),
            pltpu.SemaphoreType.DMA((8 + per,)),
            pltpu.SemaphoreType.DMA((CHUNKS,)),
            pltpu.SemaphoreType.DMA((1,)),
            pltpu.SemaphoreType.DMA((n,)),
            pltpu.SemaphoreType.DMA((levels,)),
            pltpu.SemaphoreType.DMA((levels,)),
            pltpu.SemaphoreType.DMA((levels,)),
            pltpu.SemaphoreType.DMA((levels,)),
            pltpu.SemaphoreType.DMA((1,)),
            pltpu.SemaphoreType.DMA((n,)),
        ],
        compiler_params=pltpu.CompilerParams(
            collective_id=0, has_side_effects=True, vmem_limit_bytes=48 << 20
        ),
        name="exchange",
    )(block_map, context, gates, hidden, head, teacher, tiles)


def gradient_kernel(
    inv_root,
    rows,
    cols_ref,
    scaled_ref,
    mapped_ref,
    turned_ref,
    grad_hbm,
    out_hbm,
    kl_ref,
    grad_ref,
    out_ref,
    grad_sem,
    out_sem,
):
    pieces, splits = out_sem.shape
    chunk = grad_ref.shape[1] // pieces
    span = out_ref.shape[0] // splits
    inverse = cols_ref[:, 0:1]

    def save_grad(c):
        part = pl.ds(pl.multiple_of(c * chunk, chunk), chunk)
        return pltpu.make_async_copy(grad_ref.at[:, part], grad_hbm.at[:, part], grad_sem.at[c])

    def save_out(c, r):
        part = pl.ds(pl.multiple_of(c * chunk, chunk), chunk)
        lines = pl.ds(r * span, span)
        return pltpu.make_async_copy(
            out_ref.at[lines, part], out_hbm.at[lines, part], out_sem.at[c, r]
        )

    def column(c, carry):
        part = pl.ds(pl.multiple_of(c * chunk, chunk), chunk)
        grad_ref[:, part] = (scaled_ref[:, part] - mapped_ref[:, part] * inverse).astype(
            grad_ref.dtype
        )
        for r in range(splits):
            lines = pl.ds(r * span, span)
            out_ref[lines, part] = (
                jnp.dot(turned_ref[lines, :], grad_ref[:, part], preferred_element_type=jnp.float32)
                * inv_root
            ).astype(out_ref.dtype)
            save_out(c, r).start()
        save_grad(c).start()
        return carry

    lax.fori_loop(0, pieces, column, 0)
    kl_ref[0, 0] = jnp.max(cols_ref[0:1, 1:2]) * (1.0 / rows)

    def drain(c, carry):
        for r in range(splits):
            save_out(c, r).wait()
        save_grad(c).wait()
        return carry

    lax.fori_loop(0, pieces, drain, 0)


def gradients(scaled, mapped, turned, cols, inv_root, rows):
    tokens, columns = scaled.shape
    width = turned.shape[0]
    hbm = pl.BlockSpec(memory_space=pl.ANY)
    vmem = pl.BlockSpec(memory_space=pltpu.VMEM)
    return pl.pallas_call(
        functools.partial(gradient_kernel, inv_root, rows),
        out_shape=(
            jax.ShapeDtypeStruct((tokens, columns), jnp.bfloat16),
            jax.ShapeDtypeStruct((width, columns), jnp.bfloat16),
            jax.ShapeDtypeStruct((1, 1), jnp.float32),
        ),
        in_specs=[vmem] * 4,
        out_specs=(hbm, hbm, pl.BlockSpec(memory_space=pltpu.SMEM)),
        scratch_shapes=[
            pltpu.VMEM((tokens, columns), jnp.bfloat16),
            pltpu.VMEM((width, columns), jnp.bfloat16),
            pltpu.SemaphoreType.DMA((PIECES,)),
            pltpu.SemaphoreType.DMA((PIECES, SPLITS)),
        ],
        compiler_params=pltpu.CompilerParams(vmem_limit_bytes=40 << 20),
        name="gradients",
    )(cols, scaled, mapped, turned)


def per_device(
    hidden_states, student_head, teacher_probs, block_map, context, map_gates, map_tiles
):
    voc_count = lax.axis_size("voc")
    rows_total = hidden_states.shape[0] * lax.axis_size("row")
    inv_root = 1.0 / math.sqrt(rows_total)
    vocab_total = student_head.shape[1] * voc_count
    blocks, fanout, block, _ = map_tiles.shape
    head = lax.all_gather(student_head, "row", axis=0, tiled=True)
    scaled, mapped, turned, cols = exchange(
        hidden_states,
        head,
        teacher_probs,
        block_map.T,
        context,
        map_gates.transpose(0, 2, 1),
        map_tiles.reshape(blocks * fanout, block, block),
        vocab_total,
    )
    grad_logits, head_part, kl = gradients(
        scaled, mapped, turned, cols, inv_root, rows_total
    )
    kl_loss = lax.psum(kl.reshape(()), "row")
    head_grad = lax.psum_scatter(head_part, "row", scatter_dimension=0, tiled=True)
    return (grad_logits, head_grad, kl_loss)


def solution(mesh):
    placed = (
        P("row", None),
        P("row", "voc"),
        P("row", "voc"),
        P(),
        P("row"),
        P(None, "voc", None),
        P("voc", None, None, None),
    )
    return jax.shard_map(
        per_device,
        mesh=mesh,
        in_specs=placed,
        out_specs=(P("row", "voc"), P("row", "voc"), P()),
        check_vma=False,
    )
```
